512 devices in a mesh: grp: 8 (over z_hi, core), shard: 64 (over z_lo, y, x).
Axes of the slice: x: 4, y: 8, z: 8 (z_hi: 4, z_lo: 2; z = z_hi * 2 + z_lo), core: 2. Of those that a mesh axis runs over, the one named last changes fastest.
Arguments:
- gradients: float32 [8, 1024, 512], P('grp', 'shard'), may hold values from -6 to 6
- weight: float32 [1024, 512], P('shard'), may hold values from -0.1875 to 0.1875
- moment: float32 [1024, 512], P('shard'), may hold values from -4 to 4
- second: float32 [1024, 512], P('shard'), may hold values from 0.01 to 0.5
- left_gram: float32 [1024, 1024], P('shard'), may hold values from -3 to 60, as said below
- left_basis: float32 [1024, 1024], P('shard'), may hold values from -0.1 to 1.1, as said below
- right_gram: float32 [512, 512], P('shard'), may hold values from -3 to 60, as said below
- right_basis: float32 [512, 512], P('shard'), may hold values from -0.1 to 1.1, as said below
Outputs:
- weight_new: float32 [1024, 512], P('shard')
- moment_new: float32 [1024, 512], P('shard')
- second_new: float32 [1024, 512], P('shard')
- left_new: float32 [1024, 1024], P('shard')
- left_basis_new: float32 [1024, 1024], P('shard')
- right_new: float32 [512, 512], P('shard')
- right_basis_new: float32 [512, 512], P('shard')
The draws below stay inside these ranges and needn't reach their ends.
Inputs may be any that keep to these rules, and one draw needn't show every extreme that they name: `left_gram`: symmetric positive definite. `right_gram`: symmetric positive definite. `left_basis`: square and of full rank. `right_basis`: square and of full rank.
All inputs are finite; a program needn't handle non-finite values.
Results may differ from the reference program's by a relative error of at most 0.0015.
The reference program's roundings to bfloat16 on the way count: a program that leaves them out, or rounds other values in their place, can miss the bound.
Values may be sent and summed in bfloat16 or wider, within the bound.
No kernel may reach another device: no remote copies, remote signals or barrier semaphores. Data moves between devices by JAX's collectives and lax.ppermute only.
A program may use at most 64 MiB of HBM per device.

```python
import math
import jax
import jax.numpy as jnp
from jax import lax

D = 1024
K = 512
NS_ITERS = 2
GROUPS = 8
N_GRP = 8


def gram_matrix(key, dimension):
    normal_key, scale_key = jax.random.split(key)
    gaussian = jax.random.normal(normal_key, (dimension, dimension), jnp.float32)
    symmetric = (gaussian + gaussian.T) * 0.5 ** 0.5 / math.sqrt(dimension)
    positions = jnp.arange(dimension, dtype=jnp.float32) / dimension
    scales = 4.0 * 10.0 ** positions * jax.random.uniform(scale_key, (dimension,), jnp.float32, 0.8, 1.25)
    root_scale = jnp.sqrt(scales)
    inner = jnp.eye(dimension, dtype=jnp.float32) + 0.2 * symmetric
    return root_scale[:, None] * inner * root_scale[None, :]


def near_basis(key, dimension):
    spread = 0.22 * jax.random.normal(key, (dimension, dimension), jnp.float32)
    return jnp.eye(dimension, dtype=jnp.float32) + spread / math.sqrt(dimension)


def draw_left_gram(key, part):
    return gram_matrix(jax.random.fold_in(key, 11), D)


def draw_right_gram(key, part):
    return gram_matrix(jax.random.fold_in(key, 23), K)


def draw_left_basis(key, part):
    return near_basis(jax.random.fold_in(key, 37), D)


def draw_right_basis(key, part):
    return near_basis(jax.random.fold_in(key, 41), K)


def level_of(own_key, dims, cuts, smallest, top_value):
    level = 1.0
    for position, parts in cuts:
        draws = jax.random.uniform(jax.random.fold_in(jax.random.fold_in(own_key, 6), position), (parts,), jnp.float32, smallest / len(cuts), top_value / len(cuts))
        level = level * jnp.repeat(jnp.exp(draws), dims[position] // parts).reshape((-1,) + (1,) * (len(dims) - 1 - position))
    return level


def noise(key, extent, scale, reach, cuts=(), kind=jnp.bfloat16):
    values = scale * jax.random.normal(key, extent, jnp.float32)
    if cuts:
        values = values * level_of(key, extent, cuts, -0.22, 0.18)
    return jnp.clip(values, -reach, reach).astype(kind)


def setup_inputs(seed: int = 0) -> dict:
    key_of = jax.random.split(jax.random.key(seed), 9)
    gradients = noise(key_of[0], (GROUPS, D, K), 1.0, 6.0, ((0, 8), (1, 64)), jnp.float32)
    weight = noise(key_of[1], (D, K), D ** -0.5, 0.1875, ((0, 64),), jnp.float32)
    moment = noise(key_of[2], (D, K), 0.3, 4.0, ((0, 64),), jnp.float32)
    second = jnp.clip(jnp.exp(math.log(0.5) - 3.912023 * jax.random.uniform(key_of[3], (D, K), jnp.float32) ** level_of(key_of[3], (D, K), ((0, 64),), -0.2, 0.2)), 0.01, 0.5)
    left_gram = draw_left_gram(jax.random.fold_in(key_of[8], 71), 0)
    left_basis = draw_left_basis(jax.random.fold_in(key_of[8], 71), 0)
    right_gram = draw_right_gram(jax.random.fold_in(key_of[8], 71), 0)
    right_basis = draw_right_basis(jax.random.fold_in(key_of[8], 71), 0)
    return {"gradients": gradients, "weight": weight, "moment": moment, "second": second, "left_gram": left_gram, "left_basis": left_basis, "right_gram": right_gram, "right_basis": right_basis}


BETA_ONE = 0.9
BETA_TWO = 0.95
GRAM_DECAY = 0.95
ADAM_EPS = 1e-08
NORM_EPS = 1e-06
STEP_SIZE = 0.02
START_SCALE = 0.75
PRECISE = lax.Precision.HIGHEST

def orthonormalize(power):
    column_sums = lax.optimization_barrier(jnp.sum(power * power, axis=0))
    current = lax.optimization_barrier((START_SCALE * power / jnp.sqrt(column_sums + NORM_EPS)).astype(jnp.bfloat16))
    result = power
    for sweep in range(NS_ITERS):
        square = jnp.dot(current, current.T, preferred_element_type=jnp.float32).astype(jnp.bfloat16)
        result = 1.5 * current.astype(jnp.float32) - 0.5 * jnp.dot(square, current, preferred_element_type=jnp.float32)
        current = lax.optimization_barrier(result.astype(jnp.bfloat16))
    return result

def reference(gradients, weight, moment, second, left_gram, left_basis, right_gram, right_basis):
    gradient = lax.optimization_barrier(jnp.sum(gradients, axis=0)) / N_GRP
    moment_new = BETA_ONE * moment + (1.0 - BETA_ONE) * gradient
    grad_half = gradient.astype(jnp.bfloat16)
    moment_half = moment_new.astype(jnp.bfloat16)
    left_half = lax.optimization_barrier(left_basis.astype(jnp.bfloat16))
    right_half = lax.optimization_barrier(right_basis.astype(jnp.bfloat16))
    turned_grad = jnp.dot(left_half.T, grad_half, preferred_element_type=jnp.float32).astype(jnp.bfloat16)
    turned_moment = jnp.dot(left_half.T, moment_half, preferred_element_type=jnp.float32).astype(jnp.bfloat16)
    rotated_grad = jnp.dot(turned_grad, right_half, preferred_element_type=jnp.float32)
    rotated_moment = jnp.dot(turned_moment, right_half, preferred_element_type=jnp.float32)
    second_new = BETA_TWO * second + (1.0 - BETA_TWO) * rotated_grad * rotated_grad
    direction = (rotated_moment / (jnp.sqrt(second_new) + ADAM_EPS)).astype(jnp.bfloat16)
    returned = jnp.dot(direction, right_half.T, preferred_element_type=jnp.float32).astype(jnp.bfloat16)
    update = jnp.dot(left_half, returned, preferred_element_type=jnp.float32)
    weight_new = weight - STEP_SIZE * update
    left_new = GRAM_DECAY * left_gram + (1.0 - GRAM_DECAY) * jnp.dot(grad_half, grad_half.T, preferred_element_type=jnp.float32)
    right_new = GRAM_DECAY * right_gram + (1.0 - GRAM_DECAY) * jnp.dot(grad_half.T, grad_half, preferred_element_type=jnp.float32)
    left_power = jnp.dot(left_new, left_half.astype(jnp.float32), precision=PRECISE)
    right_power = jnp.dot(right_new, right_half.astype(jnp.float32), precision=PRECISE)
    return (weight_new, moment_new, second_new, left_new, orthonormalize(left_power), right_new, orthonormalize(right_power))
```

```python
import jax
import jax.numpy as jnp
from jax import lax
from jax.sharding import Mesh, PartitionSpec as P

NS_ITERS = 2

BETA_ONE = 0.9
BETA_TWO = 0.95
GRAM_DECAY = 0.95
ADAM_EPS = 1e-08
NORM_EPS = 1e-06
STEP_SIZE = 0.02
START_SCALE = 0.75

AXES = ("zhi", "core", "zlo", "y", "x")
CUT = (4, 2, 2, 8, 4)
GRP = ("zhi", "core")
SHARD = ("zlo", "y", "x")
bf16 = jnp.bfloat16
f32 = jnp.float32


def mm(a, b, ca, cb):
    return lax.dot_general(a, b, (((ca,), (cb,)), ((), ())), preferred_element_type=f32)


def gather(value, axes, size):
    copies = jnp.broadcast_to(value[None], (size,) + value.shape)
    return lax.all_to_all(copies, axes, 0, 0)


def pair(value):
    high = lax.reduce_precision(value, 8, 7)
    return high.astype(bf16), (value - high).astype(bf16)


def newton_schulz(high, low, basis, first, count):
    power = mm(high, basis, 1, 0) + mm(low, basis, 1, 0)
    sums = jnp.sum(power * power, axis=0)
    current = lax.optimization_barrier((START_SCALE * power / jnp.sqrt(sums + NORM_EPS)).astype(bf16))
    for _ in range(NS_ITERS - 1):
        square = mm(current, current, 1, 1).astype(bf16)
        running = 1.5 * current.astype(f32) - 0.5 * mm(square, current, 1, 0)
        current = lax.optimization_barrier(running.astype(bf16))
    rows = lax.dynamic_slice_in_dim(current, first, count, 0)
    square = mm(rows, current, 1, 1).astype(bf16)
    return 1.5 * rows.astype(f32) - 0.5 * mm(square, current, 1, 0)


def local(gradients, weight, moment, second, left_gram, left_basis, right_gram, right_basis):
    n_grp = lax.axis_size(GRP)
    n_zlo, n_y, n_x = (lax.axis_size(a) for a in SHARD)
    rows, width = weight.shape
    right_rows = right_gram.shape[0]
    n_shard = n_zlo * n_y * n_x
    deep = n_shard * rows
    core = lax.axis_index("core")
    shard = lax.axis_index(SHARD)

    gradient = jnp.sum(gather(gradients[0], GRP, n_grp), axis=0) / n_grp
    moment_new = BETA_ONE * moment + (1.0 - BETA_ONE) * gradient
    grad_half = gradient.astype(bf16)
    moment_half = moment_new.astype(bf16)
    left_half = left_basis.astype(bf16)
    right_half = right_basis.astype(bf16)

    def mine(value):
        half = value.shape[1] // 2
        return jnp.where(core == 0, value[:, :half], value[:, half:])

    left_high, left_low = pair(left_gram)
    right_high, right_low = pair(right_gram)
    second_high, second_low = pair(second)
    right_pack = jnp.concatenate(
        [
            jnp.concatenate([mine(right_half), mine(right_high)], axis=0),
            jnp.concatenate([mine(right_low), mine(right_low)], axis=0),
        ],
        axis=1,
    )
    payload = jnp.stack(
        [
            mine(left_half),
            mine(left_high),
            mine(left_low),
            jnp.concatenate([mine(grad_half), mine(moment_half)], axis=1),
            jnp.concatenate([mine(second_high), mine(second_low)], axis=1),
            right_pack,
        ]
    )
    payload = gather(payload, "y", n_y)
    payload = gather(payload, ("zlo", "x"), n_zlo * n_x)
    other = lax.ppermute(payload, "core", [(0, 1), (1, 0)])
    def order(value):
        value = value.reshape(n_zlo, n_x, n_y, 6, rows, width)
        return value.transpose(3, 0, 2, 1, 4, 5)

    payload, other = order(payload), order(other)
    lower = jnp.where(core == 0, payload, other)
    upper = jnp.where(core == 0, other, payload)

    def whole(kind, which=slice(None), rows_=slice(None)):
        parts = [v[kind][..., rows_, :] for v in (lower, upper)]
        parts = [v.reshape(-1, v.shape[-1])[:, which] for v in parts]
        return jnp.concatenate(parts, axis=1)

    quarter = width // 2
    first_q, second_q = slice(0, quarter), slice(quarter, width)
    basis = whole(0)
    gram_high, gram_low = whole(1), whole(2)
    grad, mom = whole(3, first_q), whole(3, second_q)
    second_all = whole(4, first_q).astype(f32) + whole(4, second_q).astype(f32)
    right = whole(5, first_q, slice(0, right_rows))
    rgram_high = whole(5, first_q, slice(right_rows, rows))
    rgram_low = whole(5, second_q, slice(0, right_rows))

    row_first = shard * rows
    right_first = shard * right_rows

    gram = GRAM_DECAY * (gram_high.astype(f32) + gram_low.astype(f32)) + (1.0 - GRAM_DECAY) * mm(grad, grad, 1, 1)
    left_new = GRAM_DECAY * left_gram + (1.0 - GRAM_DECAY) * mm(grad_half, grad, 1, 1)
    left_result = newton_schulz(*pair(gram), basis, row_first, rows)
    rgram = GRAM_DECAY * (rgram_high.astype(f32) + rgram_low.astype(f32)) + (1.0 - GRAM_DECAY) * mm(grad, grad, 0, 0)
    grad_columns = lax.dynamic_slice_in_dim(grad, right_first, right_rows, 1)
    right_new = GRAM_DECAY * right_gram + (1.0 - GRAM_DECAY) * mm(grad_columns, grad, 0, 0)
    right_result = newton_schulz(*pair(rgram), right, right_first, right_rows)
    turned_grad = mm(basis, grad, 0, 0).astype(bf16)
    turned_moment = mm(basis, mom, 0, 0).astype(bf16)
    rotated_grad = mm(turned_grad, right, 1, 0)
    rotated_moment = mm(turned_moment, right, 1, 0)
    second_full = BETA_TWO * second_all + (1.0 - BETA_TWO) * rotated_grad * rotated_grad
    own_rotated = lax.dynamic_slice_in_dim(rotated_grad, row_first, rows, 0)
    second_new = BETA_TWO * second + (1.0 - BETA_TWO) * own_rotated * own_rotated
    direction = (rotated_moment / (jnp.sqrt(second_full) + ADAM_EPS)).astype(bf16)
    returned = mm(direction, right, 1, 1).astype(bf16)
    weight_new = weight - STEP_SIZE * mm(left_half, returned, 1, 0)
    return (weight_new, moment_new, second_new, left_new, left_result, right_new, right_result)


def solution(mesh):
    cut = Mesh(mesh.devices.reshape(CUT), AXES)
    rowwise = P(SHARD, None)
    return jax.shard_map(
        local,
        mesh=cut,
        in_specs=(P(GRP, SHARD, None),) + (rowwise,) * 7,
        out_specs=(rowwise,) * 7,
        check_vma=False,
    )
```

```python
import jax
import jax.numpy as jnp
from jax import lax
from jax.experimental import pallas as pl
from jax.experimental.pallas import tpu as pltpu
from jax.sharding import Mesh, PartitionSpec as P

NS_ITERS = 2

BETA_ONE = 0.9
BETA_TWO = 0.95
GRAM_DECAY = 0.95
ADAM_EPS = 1e-08
NORM_EPS = 1e-06
STEP_SIZE = 0.02
START_SCALE = 0.75

AXES = ("zhi", "core", "zlo", "y", "x")
CUT = (4, 2, 2, 8, 4)
GRP = ("zhi", "core")
SHARD = ("zlo", "y", "x")
NZ, NY, NX = CUT[2:]
bf16 = jnp.bfloat16
f32 = jnp.float32

BLOCK = 128
BLOCKS = 8
SENT = BLOCKS // 2 + 1


def mm(a, b, ca, cb):
    return lax.dot_general(a, b, (((ca,), (cb,)), ((), ())), preferred_element_type=f32)


def gather(value, axes, size):
    copies = jnp.broadcast_to(value[None], (size,) + value.shape)
    return lax.all_to_all(copies, axes, 0, 0)


def pair(value):
    high = lax.reduce_precision(value, 8, 7)
    return high.astype(bf16), (value - high).astype(bf16)


def split(value):
    high = value.astype(bf16)
    return high, (value - high.astype(f32)).astype(bf16)


def refresh(power_tile, n_tiles, tile, first, count, power, start, current, out_ref):
    sums = None
    for t in range(n_tiles):
        p = power_tile(t)
        power[pl.ds(t * tile, tile), :] = p
        s = jnp.sum(p * p, axis=0, keepdims=True)
        sums = s if sums is None else sums + s
    scale = START_SCALE / jnp.sqrt(sums + NORM_EPS)
    for t in range(n_tiles):
        at = pl.ds(t * tile, tile)
        start[at, :] = (power[at, :] * scale).astype(bf16)
    x = start[...]
    for t in range(n_tiles):
        at = pl.ds(t * tile, tile)
        mine = start[at, :]
        square = mm(mine, x, 1, 1).astype(bf16)
        current[at, :] = (1.5 * mine.astype(f32) - 0.5 * mm(square, x, 1, 0)).astype(bf16)
    x = current[...]
    rows = current[pl.ds(pl.multiple_of(first, count), count), :]
    square = mm(rows, x, 1, 1).astype(bf16)
    out_ref[...] = 1.5 * rows.astype(f32) - 0.5 * mm(square, x, 1, 0)


def left_kernel(first_ref, mine_ref, other_ref, grad_ref, basis_ref, out_ref, gram, power, start, current):
    rows = mine_ref.shape[3]
    for r in range(BLOCKS):
        zlo, y2 = r // (BLOCKS // NZ), r % (BLOCKS // NZ)
        for j in range(SENT):
            c = (r + j) % BLOCKS
            pieces = []
            for y in (2 * y2, 2 * y2 + 1):
                for x in range(NX):
                    a = mine_ref[zlo, x, y, :, j * BLOCK : (j + 1) * BLOCK].astype(f32)
                    b = other_ref[zlo, x, y, :, j * BLOCK : (j + 1) * BLOCK].astype(f32)
                    pieces.append(a + b)
            block = GRAM_DECAY * jnp.concatenate(pieces, axis=0)
            gram[r * BLOCK : (r + 1) * BLOCK, c * BLOCK : (c + 1) * BLOCK] = block
            if 0 < j < BLOCKS // 2:
                gram[c * BLOCK : (c + 1) * BLOCK, r * BLOCK : (r + 1) * BLOCK] = block.T
    grad = grad_ref[...]
    basis = basis_ref[...]
    tile = 256

    def power_tile(t):
        at = pl.ds(t * tile, tile)
        whole = gram[at, :] + (1.0 - GRAM_DECAY) * mm(grad_ref[at, :], grad, 1, 1)
        high, low = split(whole)
        return mm(high, basis, 1, 0) + mm(low, basis, 1, 0)

    refresh(power_tile, gram.shape[0] // tile, tile, first_ref[0], rows, power, start, current, out_ref)


def left_call(first, mine, other, grad, basis, rows):
    deep = basis.shape[0]
    vmem = pl.BlockSpec(memory_space=pltpu.VMEM)
    return pl.pallas_call(
        left_kernel,
        out_shape=jax.ShapeDtypeStruct((rows, deep), f32),
        in_specs=[pl.BlockSpec(memory_space=pltpu.SMEM)] + [vmem] * 4,
        out_specs=vmem,
        scratch_shapes=[
            pltpu.VMEM((deep, deep), f32),
            pltpu.VMEM((deep, deep), f32),
            pltpu.VMEM((deep, deep), bf16),
            pltpu.VMEM((deep, deep), bf16),
        ],
        compiler_params=pltpu.CompilerParams(vmem_limit_bytes=40 << 20),
        name="left_refresh",
    )(first, mine, other, grad, basis)


def right_kernel(first_ref, gram_ref, grad_ref, basis_ref, out_ref, power, start, current):
    rows = out_ref.shape[0]
    basis = basis_ref[...]
    grad = grad_ref[...]
    tile = 256

    def power_tile(t):
        at = pl.ds(t * tile, tile)
        whole = GRAM_DECAY * gram_ref[at, :] + (1.0 - GRAM_DECAY) * mm(grad_ref[:, t * tile : (t + 1) * tile], grad, 0, 0)
        high, low = split(whole)
        return mm(high, basis, 1, 0) + mm(low, basis, 1, 0)

    refresh(power_tile, gram_ref.shape[0] // tile, tile, first_ref[0], rows, power, start, current, out_ref)


def right_call(first, gram, grad, basis, rows):
    width = basis.shape[0]
    vmem = pl.BlockSpec(memory_space=pltpu.VMEM)
    return pl.pallas_call(
        right_kernel,
        out_shape=jax.ShapeDtypeStruct((rows, width), f32),
        in_specs=[pl.BlockSpec(memory_space=pltpu.SMEM)] + [vmem] * 3,
        out_specs=vmem,
        scratch_shapes=[
            pltpu.VMEM((width, width), f32),
            pltpu.VMEM((width, width), bf16),
            pltpu.VMEM((width, width), bf16),
        ],
        compiler_params=pltpu.CompilerParams(vmem_limit_bytes=16 << 20),
        name="right_refresh",
    )(first, gram, grad, basis)


def local(gradients, weight, moment, second, left_gram, left_basis, right_gram, right_basis):
    n_grp = CUT[0] * CUT[1]
    rows, width = weight.shape
    right_rows = right_gram.shape[0]
    n_shard = NZ * NY * NX
    deep = n_shard * rows
    core = lax.axis_index("core")
    group = lax.axis_index(GRP)
    shard = lax.axis_index(SHARD)
    row_first = shard * rows
    right_first = shard * right_rows
    first = core == 0

    gradient = jnp.sum(gather(gradients[0], GRP, n_grp), axis=0) / n_grp
    moment_new = BETA_ONE * moment + (1.0 - BETA_ONE) * gradient
    grad_half = gradient.astype(bf16)
    moment_half = moment_new.astype(bf16)
    left_half = left_basis.astype(bf16)
    right_half = right_basis.astype(bf16)

    def fold(value, parts):
        return jnp.concatenate(jnp.split(value, parts, axis=1), axis=0)

    share = rows // n_grp
    own_second = jnp.concatenate([fold(v, 4) for v in pair(lax.dynamic_slice_in_dim(second, group * share, share, 0))], axis=0)
    start = (shard // (n_shard // BLOCKS)) * BLOCK
    round_gram = jnp.concatenate([left_gram, left_gram[:, : (SENT - 1) * BLOCK]], axis=1)
    sent_gram = lax.dynamic_slice_in_dim(round_gram, start, SENT * BLOCK, 1)
    half = deep // 2
    payload = jnp.concatenate(
        [
            jnp.where(first, left_half[:, :half], left_half[:, half:]),
            jnp.where(first, grad_half, moment_half),
            fold(jnp.where(first, right_half[:, : width // 2], right_half[:, width // 2 :]), 2),
            fold(jnp.where(first, *pair(right_gram)), 2),
            own_second,
            jnp.where(first, *pair(sent_gram)),
        ],
        axis=1,
    )
    cut = payload.shape[1] - SENT * BLOCK
    payload = gather(payload, "y", NY)
    early = gather(payload[..., :cut], ("zlo", "x"), NZ * NX)
    swap = [(0, 1), (1, 0)]
    shared = early[..., : cut - 128]
    shared_other = lax.ppermute(shared, "core", swap)
    late = gather(payload[..., cut:], ("zlo", "x"), NZ * NX)
    late_other = lax.ppermute(late, "core", swap)

    def order(value):
        value = value.reshape((NZ, NX) + value.shape[1:])
        return value.transpose(0, 2, 1, 3, 4)

    def unfold(value, parts):
        value = jnp.concatenate(jnp.split(value, parts, axis=-2), axis=-1)
        return value.reshape(-1, value.shape[-1])

    def lanes(at, n):
        return order(shared[..., at : at + n]), order(shared_other[..., at : at + n])

    basis = jnp.concatenate([v.reshape(deep, half) for v in lanes(0, half)], axis=1)
    a, b = (v.reshape(deep, width) for v in lanes(half, width))
    grad, mom = jnp.where(first, a, b), jnp.where(first, b, a)
    a, b = (unfold(v, 2) for v in lanes(half + width, width // 4))
    right = jnp.where(first, jnp.concatenate([a, b], axis=1), jnp.concatenate([b, a], axis=1))
    a, b = (unfold(v, 2) for v in lanes(half + width + width // 4, width // 2))
    rgram = a.astype(f32) + b.astype(f32)
    second_parts = early[..., cut - 128 :]
    n_part = rows // 2
    second_rows = unfold(second_parts[..., :n_part, :], 4).astype(f32) + unfold(second_parts[..., n_part:, :], 4).astype(f32)

    mine_rows = n_shard * share
    q = lax.broadcasted_iota(jnp.int32, (deep, mine_rows), 1)
    column = (lax.broadcasted_iota(jnp.int32, (deep, mine_rows), 0) + core * half) % deep
    zx, y, r = q // (NY * share), (q // share) % NY, q % share
    wanted = ((zx // NX * NY + y) * NX + zx % NX) * rows + group * share + r
    pick = (column == wanted).astype(bf16)
    q = lax.broadcasted_iota(jnp.int32, (deep, rows), 1)
    column = (lax.broadcasted_iota(jnp.int32, (deep, rows), 0) + core * half) % deep
    pick_own = (column == row_first + q).astype(bf16)
    left_columns = mm(basis, jnp.concatenate([pick, pick_own], axis=1), 1, 0).astype(bf16)
    turned_grad = mm(left_columns, grad, 0, 0).astype(bf16)
    turned_moment = mm(left_columns[:, :mine_rows], mom, 0, 0).astype(bf16)
    rotated_grad = mm(turned_grad, right, 1, 0)
    rotated_moment = mm(turned_moment, right, 1, 0)
    part_grad, own_grad = rotated_grad[:mine_rows], rotated_grad[mine_rows:]
    second_part = BETA_TWO * second_rows + (1.0 - BETA_TWO) * part_grad * part_grad
    second_new = BETA_TWO * second + (1.0 - BETA_TWO) * own_grad * own_grad
    direction = (rotated_moment / (jnp.sqrt(second_part) + ADAM_EPS)).astype(bf16)
    returned = mm(direction, right, 1, 1).astype(bf16)
    left_rows = jnp.where(first, left_half, jnp.concatenate([left_half[:, half:], left_half[:, :half]], axis=1))
    left_rows = mm(left_rows, pick, 1, 0).astype(bf16)
    update = jnp.sum(gather(mm(left_rows, returned, 1, 0), GRP, n_grp), axis=0)
    weight_new = weight - STEP_SIZE * update

    left_new = GRAM_DECAY * left_gram + (1.0 - GRAM_DECAY) * mm(grad_half, grad, 1, 1)
    grad_columns = lax.dynamic_slice_in_dim(grad, right_first, right_rows, 1)
    right_new = GRAM_DECAY * right_gram + (1.0 - GRAM_DECAY) * mm(grad_columns, grad, 0, 0)
    right_result = right_call((right_first // rows * rows)[None], rgram, grad, right, rows)
    right_result = lax.dynamic_slice_in_dim(right_result, right_first % rows, right_rows, 0)

    five = lambda v: v.reshape((NZ, NX) + v.shape[1:])
    left_result = left_call(row_first[None], five(late), five(late_other), grad, basis, rows)
    swapped = jnp.concatenate([left_result[:, half:], left_result[:, :half]], axis=1)
    left_result = jnp.where(first, left_result, swapped)
    return (weight_new, moment_new, second_new, left_new, left_result, right_new, right_result)


def solution(mesh):
    cut = Mesh(mesh.devices.reshape(CUT), AXES)
    rowwise = P(SHARD, None)
    return jax.shard_map(
        local,
        mesh=cut,
        in_specs=(P(GRP, SHARD, None),) + (rowwise,) * 7,
        out_specs=(rowwise,) * 7,
        check_vma=False,
    )
```

```python
import jax
import jax.numpy as jnp
from jax import lax
from jax.experimental import pallas as pl
from jax.experimental.pallas import tpu as pltpu
from jax.sharding import Mesh, PartitionSpec as P

NS_ITERS = 2

BETA_ONE = 0.9
BETA_TWO = 0.95
GRAM_DECAY = 0.95
ADAM_EPS = 1e-08
NORM_EPS = 1e-06
STEP_SIZE = 0.02
START_SCALE = 0.75

AXES = ("zhi", "core", "zlo", "yhi", "ylo", "x")
CUT = (4, 2, 2, 4, 2, 4)
GRP = ("zhi", "core")
SHARD = ("zlo", "yhi", "ylo", "x")
NEAR = ("zlo", "ylo", "x")
NZ, NF, NY, NX = CUT[2:]
bf16 = jnp.bfloat16
f32 = jnp.float32

BLOCK = 128
BLOCKS = 8
SENT = BLOCKS // 2 + 1


def mm(a, b, ca, cb):
    return lax.dot_general(a, b, (((ca,), (cb,)), ((), ())), preferred_element_type=f32)


def gather(value, axes, size):
    copies = jnp.broadcast_to(value[None], (size,) + value.shape)
    return lax.all_to_all(copies, axes, 0, 0)


def pair(value):
    high = lax.reduce_precision(value, 8, 7)
    return high.astype(bf16), (value - high).astype(bf16)


def split(value):
    high = value.astype(bf16)
    return high, (value - high.astype(f32)).astype(bf16)


def refresh(power_tile, n_tiles, tile, first, count, power, start, current, out_ref):
    sums = None
    for t in range(n_tiles):
        p = power_tile(t)
        power[pl.ds(t * tile, tile), :] = p
        s = jnp.sum(p * p, axis=0, keepdims=True)
        sums = s if sums is None else sums + s
    scale = START_SCALE / jnp.sqrt(sums + NORM_EPS)
    for t in range(n_tiles):
        at = pl.ds(t * tile, tile)
        start[at, :] = (power[at, :] * scale).astype(bf16)
    x = start[...]
    for t in range(n_tiles):
        at = pl.ds(t * tile, tile)
        mine = start[at, :]
        square = mm(mine, x, 1, 1).astype(bf16)
        current[at, :] = (1.5 * mine.astype(f32) - 0.5 * mm(square, x, 1, 0)).astype(bf16)
    x = current[...]
    rows = current[pl.ds(pl.multiple_of(first, count), count), :]
    square = mm(rows, x, 1, 1).astype(bf16)
    out_ref[...] = 1.5 * rows.astype(f32) - 0.5 * mm(square, x, 1, 0)


def left_kernel(first_ref, mine_ref, other_ref, grad_ref, basis_ref, out_ref, gram, power, start, current):
    rows = mine_ref.shape[-2]
    for r in range(BLOCKS):
        zlo, far = r // NF, r % NF
        for j in range(SENT):
            c = (r + j) % BLOCKS
            at = pl.ds(j * BLOCK, BLOCK)
            pieces = []
            for near in range(NY * NX):
                place = (zlo, near // NX, near % NX, far, slice(None), at)
                pieces.append(mine_ref[place].astype(f32) + other_ref[place].astype(f32))
            block = GRAM_DECAY * jnp.concatenate(pieces, axis=0)
            gram[r * BLOCK : (r + 1) * BLOCK, c * BLOCK : (c + 1) * BLOCK] = block
            if 0 < j < BLOCKS // 2:
                gram[c * BLOCK : (c + 1) * BLOCK, r * BLOCK : (r + 1) * BLOCK] = block.T
    grad = grad_ref[...]
    basis = basis_ref[...]
    tile = 256

    def power_tile(t):
        at = pl.ds(t * tile, tile)
        whole = gram[at, :] + (1.0 - GRAM_DECAY) * mm(grad_ref[at, :], grad, 1, 1)
        high, low = split(whole)
        return mm(high, basis, 1, 0) + mm(low, basis, 1, 0)

    refresh(power_tile, gram.shape[0] // tile, tile, first_ref[0], rows, power, start, current, out_ref)


def left_call(first, mine, other, grad, basis, rows):
    deep = basis.shape[0]
    vmem = pl.BlockSpec(memory_space=pltpu.VMEM)
    return pl.pallas_call(
        left_kernel,
        out_shape=jax.ShapeDtypeStruct((rows, deep), f32),
        in_specs=[pl.BlockSpec(memory_space=pltpu.SMEM)] + [vmem] * 4,
        out_specs=vmem,
        scratch_shapes=[
            pltpu.VMEM((deep, deep), f32),
            pltpu.VMEM((deep, deep), f32),
            pltpu.VMEM((deep, deep), bf16),
            pltpu.VMEM((deep, deep), bf16),
        ],
        compiler_params=pltpu.CompilerParams(vmem_limit_bytes=40 << 20),
        cost_estimate=pl.CostEstimate(flops=10 * deep**3, transcendentals=deep, bytes_accessed=8 * deep**2),
        name="left_refresh",
    )(first, mine, other, grad, basis)


def mid_kernel(
    at_ref, mine_ref, other_ref, second_rows_ref, second_ref, left_rows_ref, left_gram_ref,
    basis_ref, grad_ref, update_ref, second_new_ref, left_new_ref, right_term_ref, right_out_ref,
    mom, right, rgram, power, start, current,
):
    core, group, row_first, right_first = (at_ref[i] for i in range(4))
    first = core == 0
    rows, width = second_ref.shape
    deep = basis_ref.shape[0]
    half = deep // 2
    share = second_rows_ref.shape[0] // (deep // rows)
    right_rows = rows // 2
    spot = 0
    for zlo in range(NZ):
        for far in range(NF):
            for y in range(NY):
                for x in range(NX):
                    def lanes(at, n):
                        place = (zlo, y, x, far, slice(None), pl.ds(at, n))
                        return mine_ref[place], other_ref[place]

                    to = pl.ds(spot * rows, rows)
                    a, b = lanes(0, half)
                    basis_ref[to, :half] = a
                    basis_ref[to, half:] = b
                    a, b = lanes(half, width)
                    grad_ref[to, :] = jnp.where(first, a, b)
                    mom[to, :] = jnp.where(first, b, a)
                    to = pl.ds(spot * right_rows, right_rows)
                    n = width // 4
                    a, b = (v.astype(f32) for v in lanes(half + width, n))
                    low, high = jnp.where(first, a, b), jnp.where(first, b, a)
                    for part in range(2):
                        of = slice(part * right_rows, (part + 1) * right_rows)
                        right[to, part * n : (part + 1) * n] = low[of]
                        right[to, (2 + part) * n : (3 + part) * n] = high[of]
                    a, b = lanes(half + width + n, 2 * n)
                    both = GRAM_DECAY * (a.astype(f32) + b.astype(f32))
                    for part in range(2):
                        of = slice(part * right_rows, (part + 1) * right_rows)
                        rgram[to, part * 2 * n : (part + 1) * 2 * n] = both[of]
                    spot += 1
    basis, grad = basis_ref[...], grad_ref[...]
    rbasis = right[...].astype(bf16)

    n = second_rows_ref.shape[0]
    q = lax.broadcasted_iota(jnp.int32, (1, n), 1)
    r, far, near = q % share, (q // share) % NF, q // (share * NF)
    wanted = ((near // (NY * NX) * NF + far) * (NY * NX) + near % (NY * NX)) * rows + group * share + r
    column = (lax.broadcasted_iota(jnp.int32, (deep, n), 0) + core * half) % deep
    pick = jnp.where(column == wanted, 1.0, 0.0).astype(bf16)
    q = lax.broadcasted_iota(jnp.int32, (1, n), 1)
    own = jnp.where((column == row_first + q) & (q < rows), 1.0, 0.0).astype(bf16)
    columns = mm(basis, pick, 1, 0).astype(bf16)
    own_columns = mm(basis, own, 1, 0).astype(bf16)
    rotated_grad = mm(mm(columns, grad, 0, 0).astype(bf16), rbasis, 1, 0)
    rotated_moment = mm(mm(columns, mom[...], 0, 0).astype(bf16), rbasis, 1, 0)
    own_grad = mm(mm(own_columns, grad, 0, 0).astype(bf16), rbasis, 1, 0)[:rows]
    second_part = BETA_TWO * second_rows_ref[...] + (1.0 - BETA_TWO) * rotated_grad * rotated_grad
    second_new_ref[...] = BETA_TWO * second_ref[...] + (1.0 - BETA_TWO) * own_grad * own_grad
    direction = (rotated_moment / (jnp.sqrt(second_part) + ADAM_EPS)).astype(bf16)
    returned = mm(direction, rbasis, 1, 1).astype(bf16)
    own_rows = left_rows_ref[...]
    own_rows = jnp.where(first, own_rows, jnp.concatenate([own_rows[:, half:], own_rows[:, :half]], axis=1))
    update_ref[...] = mm(mm(own_rows, pick, 1, 0).astype(bf16), returned, 1, 0)

    own_grad = grad_ref[pl.ds(pl.multiple_of(row_first, rows), rows), :]
    left_new_ref[...] = GRAM_DECAY * left_gram_ref[...] + (1.0 - GRAM_DECAY) * mm(own_grad, grad, 1, 1)
    q = lax.broadcasted_iota(jnp.int32, (width, BLOCK), 1)
    column = lax.broadcasted_iota(jnp.int32, (width, BLOCK), 0)
    own = jnp.where((column == right_first + q) & (q < rows), 1.0, 0.0).astype(bf16)
    right_term_ref[...] = mm(mm(grad, own, 1, 0).astype(bf16), grad, 0, 0)[:rows]

    tile = 256

    def power_tile(t):
        at = pl.ds(t * tile, tile)
        whole = rgram[at, :] + (1.0 - GRAM_DECAY) * mm(grad_ref[:, t * tile : (t + 1) * tile], grad, 0, 0)
        high, low = split(whole)
        return mm(high, rbasis, 1, 0) + mm(low, rbasis, 1, 0)

    refresh(power_tile, width // tile, tile, right_first, rows, power, start, current, right_out_ref)


def mid_call(at, mine, other, second_rows, second, left_rows, left_gram):
    rows, deep = left_rows.shape
    width = second.shape[1]
    vmem = pl.BlockSpec(memory_space=pltpu.VMEM)
    shapes = [
        ((deep, deep), bf16), ((deep, width), bf16), ((rows, width), f32), ((rows, width), f32),
        ((rows, deep), f32), ((rows, width), f32), ((rows, width), f32),
    ]
    return pl.pallas_call(
        mid_kernel,
        out_shape=[jax.ShapeDtypeStruct(*v) for v in shapes],
        in_specs=[pl.BlockSpec(memory_space=pltpu.SMEM)] + [vmem] * 6,
        out_specs=[vmem] * len(shapes),
        scratch_shapes=[
            pltpu.VMEM((deep, width), bf16),
            pltpu.VMEM((width, width), f32),
            pltpu.VMEM((width, width), f32),
            pltpu.VMEM((width, width), f32),
            pltpu.VMEM((width, width), bf16),
            pltpu.VMEM((width, width), bf16),
        ],
        compiler_params=pltpu.CompilerParams(vmem_limit_bytes=40 << 20),
        cost_estimate=pl.CostEstimate(flops=6 * deep**3, transcendentals=width**2, bytes_accessed=12 * deep**2),
        name="middle",
    )(at, mine, other, second_rows, second, left_rows, left_gram)


def local(gradients, weight, moment, second, left_gram, left_basis, right_gram, right_basis):
    n_grp = CUT[0] * CUT[1]
    rows, width = weight.shape
    right_rows = right_gram.shape[0]
    n_shard = NZ * NF * NY * NX
    deep = n_shard * rows
    core = lax.axis_index("core")
    group = lax.axis_index(GRP)
    shard = lax.axis_index(SHARD)
    row_first = shard * rows
    right_first = shard * right_rows
    first = core == 0

    gradient = jnp.sum(gather(gradients[0], GRP, n_grp), axis=0) / n_grp
    moment_new = BETA_ONE * moment + (1.0 - BETA_ONE) * gradient
    grad_half = gradient.astype(bf16)
    moment_half = moment_new.astype(bf16)
    left_half = left_basis.astype(bf16)
    right_half = right_basis.astype(bf16)

    def fold(value, parts):
        return jnp.concatenate(jnp.split(value, parts, axis=1), axis=0)

    share = rows // n_grp
    own_second = jnp.concatenate([fold(v, 4) for v in pair(lax.dynamic_slice_in_dim(second, group * share, share, 0))], axis=0)
    start = (shard // (n_shard // BLOCKS)) * BLOCK
    round_gram = jnp.concatenate([left_gram, left_gram[:, : (SENT - 1) * BLOCK]], axis=1)
    sent_gram = lax.dynamic_slice_in_dim(round_gram, start, SENT * BLOCK, 1)
    half = deep // 2
    payload = jnp.concatenate(
        [
            jnp.where(first, left_half[:, :half], left_half[:, half:]),
            jnp.where(first, grad_half, moment_half),
            fold(jnp.where(first, right_half[:, : width // 2], right_half[:, width // 2 :]), 2),
            fold(jnp.where(first, *pair(right_gram)), 2),
            own_second,
            jnp.where(first, *pair(sent_gram)),
        ],
        axis=1,
    )
    cut = payload.shape[1] - SENT * BLOCK
    payload = gather(payload, "yhi", NF)
    near = NZ * NY * NX
    parted = lambda v: v.reshape((NZ, NY, NX) + v.shape[1:])
    swap = [(0, 1), (1, 0)]
    early = gather(payload[..., :cut], NEAR, near)
    early_other = lax.ppermute(early, "core", swap)
    late = gather(payload[..., cut:], NEAR, near)

    second_parts = early[..., cut - 128 :].astype(f32)
    second_parts = second_parts[..., : rows // 2, :] + second_parts[..., rows // 2 :, :]
    second_rows = jnp.concatenate(jnp.split(second_parts, 4, axis=-2), axis=-1).reshape(-1, width)

    at = jnp.stack([core, group, row_first, right_first // rows * rows]).astype(jnp.int32)
    results = mid_call(at, parted(early), parted(early_other), second_rows, second, left_half, left_gram)
    results, late = lax.optimization_barrier((results, late))
    basis, grad, update, second_new, left_new, right_term, right_result = results
    late_other = lax.ppermute(late, "core", swap)
    updates = gather(update, GRP, n_grp)
    own = lambda v: lax.dynamic_slice_in_dim(v, right_first % rows, right_rows, 0)
    right_new = GRAM_DECAY * right_gram + (1.0 - GRAM_DECAY) * own(right_term)
    right_result = own(right_result)
    left_result = left_call(row_first[None], parted(late), parted(late_other), grad, basis, rows)
    updates, left_result = lax.optimization_barrier((updates, left_result))
    weight_new = weight - STEP_SIZE * jnp.sum(updates, axis=0)
    swapped = jnp.concatenate([left_result[:, half:], left_result[:, :half]], axis=1)
    left_result = jnp.where(first, left_result, swapped)
    return (weight_new, moment_new, second_new, left_new, left_result, right_new, right_result)


def solution(mesh):
    cut = Mesh(mesh.devices.reshape(CUT), AXES)
    rowwise = P(SHARD, None)
    return jax.shard_map(
        local,
        mesh=cut,
        in_specs=(P(GRP, SHARD, None),) + (rowwise,) * 7,
        out_specs=(rowwise,) * 7,
        check_vma=False,
    )
```

```python
import itertools

import jax
import jax.numpy as jnp
import numpy as np
from jax import lax
from jax.experimental import pallas as pl
from jax.experimental.pallas import tpu as pltpu
from jax.sharding import Mesh, PartitionSpec as P

NS_ITERS = 2

BETA_ONE = 0.9
BETA_TWO = 0.95
GRAM_DECAY = 0.95
ADAM_EPS = 1e-08
NORM_EPS = 1e-06
STEP_SIZE = 0.02
START_SCALE = 0.75

AXES = ("zhi", "core", "zlo", "yhi", "ylo", "xhi", "xlo")
CUT = (4, 2, 2, 4, 2, 2, 2)
GRP = ("zhi", "core")
SHARD = ("zlo", "yhi", "ylo", "xhi", "xlo")
NZ, NF, NY, NXF, NXN = CUT[2:]
NX = NXF * NXN
NEAR = (NZ, NY, NXN)
bf16 = jnp.bfloat16
f32 = jnp.float32

BLOCK = 128
BLOCKS = 8
SENT = BLOCKS // 2 + 1


def mm(a, b, ca, cb):
    return lax.dot_general(a, b, (((ca,), (cb,)), ((), ())), preferred_element_type=f32)


def cubes():
    groups = []
    deep, high, wide = CUT[0] * NZ, NF * NY, NX
    for core in range(CUT[1]):
        for corner in itertools.product(range(0, deep, 2), range(0, high, 2), range(0, wide, 2)):
            group = {}
            for step in itertools.product(range(2), repeat=3):
                z, y, x = (
                    (a + core + b) % n for a, b, n in zip(corner, step, (deep, high, wide))
                )
                place = (z // NZ, core, z % NZ, y // NY, y % NY, x // NXN, x % NXN)
                group[z % NZ, y % NY, x % NXN] = int(np.ravel_multi_index(place, CUT))
            groups.append([group[k] for k in sorted(group)])
    return groups


def gather(value, axes, size, groups=None):
    copies = jnp.broadcast_to(value[None], (size,) + value.shape)
    return lax.all_to_all(copies, axes, 0, 0, axis_index_groups=groups)


def pair(value):
    high = lax.reduce_precision(value, 8, 7)
    return high.astype(bf16), (value - high).astype(bf16)


def split(value):
    high = value.astype(bf16)
    return high, (value - high.astype(f32)).astype(bf16)


def refresh(power_tile, n_tiles, tile, first, count, power, start, current, out_ref):
    sums = None
    for t in range(n_tiles):
        p = power_tile(t)
        power[pl.ds(t * tile, tile), :] = p
        s = jnp.sum(p * p, axis=0, keepdims=True)
        sums = s if sums is None else sums + s
    scale = START_SCALE / jnp.sqrt(sums + NORM_EPS)
    for t in range(n_tiles):
        at = pl.ds(t * tile, tile)
        start[at, :] = (power[at, :] * scale).astype(bf16)
    x = start[...]
    for t in range(n_tiles):
        at = pl.ds(t * tile, tile)
        mine = start[at, :]
        square = mm(mine, x, 1, 1).astype(bf16)
        current[at, :] = (1.5 * mine.astype(f32) - 0.5 * mm(square, x, 1, 0)).astype(bf16)
    x = current[...]
    rows = current[pl.ds(pl.multiple_of(first, count), count), :]
    square = mm(rows, x, 1, 1).astype(bf16)
    out_ref[...] = 1.5 * rows.astype(f32) - 0.5 * mm(square, x, 1, 0)


def left_kernel(first_ref, mine_ref, other_ref, grad_ref, basis_ref, out_ref, gram, power, start, current):
    rows = mine_ref.shape[-2]
    for r in range(BLOCKS):
        zlo, far = r // NF, r % NF
        for j in range(SENT):
            c = (r + j) % BLOCKS
            at = pl.ds(j * BLOCK, BLOCK)
            pieces = []
            for near in range(NY * NX):
                y, x = near // NX, near % NX
                place = (zlo, y, x % NXN, x // NXN, far, slice(None), at)
                pieces.append(mine_ref[place].astype(f32) + other_ref[place].astype(f32))
            block = GRAM_DECAY * jnp.concatenate(pieces, axis=0)
            gram[r * BLOCK : (r + 1) * BLOCK, c * BLOCK : (c + 1) * BLOCK] = block
            if 0 < j < BLOCKS // 2:
                gram[c * BLOCK : (c + 1) * BLOCK, r * BLOCK : (r + 1) * BLOCK] = block.T
    grad = grad_ref[...]
    basis = basis_ref[...]
    tile = 256

    def power_tile(t):
        at = pl.ds(t * tile, tile)
        whole = gram[at, :] + (1.0 - GRAM_DECAY) * mm(grad_ref[at, :], grad, 1, 1)
        high, low = split(whole)
        return mm(high, basis, 1, 0) + mm(low, basis, 1, 0)

    refresh(power_tile, gram.shape[0] // tile, tile, first_ref[0], rows, power, start, current, out_ref)


def left_call(first, mine, other, grad, basis, rows):
    deep = basis.shape[0]
    vmem = pl.BlockSpec(memory_space=pltpu.VMEM)
    return pl.pallas_call(
        left_kernel,
        out_shape=jax.ShapeDtypeStruct((rows, deep), f32),
        in_specs=[pl.BlockSpec(memory_space=pltpu.SMEM)] + [vmem] * 4,
        out_specs=vmem,
        scratch_shapes=[
            pltpu.VMEM((deep, deep), f32),
            pltpu.VMEM((deep, deep), f32),
            pltpu.VMEM((deep, deep), bf16),
            pltpu.VMEM((deep, deep), bf16),
        ],
        compiler_params=pltpu.CompilerParams(vmem_limit_bytes=40 << 20),
        cost_estimate=pl.CostEstimate(flops=10 * deep**3, transcendentals=deep, bytes_accessed=8 * deep**2),
        name="left_refresh",
    )(first, mine, other, grad, basis)


def mid_kernel(
    at_ref, mine_ref, other_ref, second_rows_ref, second_ref, left_rows_ref, left_gram_ref,
    basis_ref, grad_ref, update_ref, second_new_ref, left_new_ref, right_term_ref, right_out_ref,
    mom, right, rgram, power, start, current,
):
    core, group, row_first, right_first = (at_ref[i] for i in range(4))
    first = core == 0
    rows, width = second_ref.shape
    deep = basis_ref.shape[0]
    half = deep // 2
    share = second_rows_ref.shape[0] // (deep // rows)
    right_rows = rows // 2
    spot = 0
    for zlo in range(NZ):
        for far in range(NF):
            for y in range(NY):
                for x in range(NX):
                    def lanes(at, n):
                        place = (zlo, y, x % NXN, x // NXN, far, slice(None), pl.ds(at, n))
                        return mine_ref[place], other_ref[place]

                    to = pl.ds(spot * rows, rows)
                    a, b = lanes(0, half)
                    basis_ref[to, :half] = a
                    basis_ref[to, half:] = b
                    a, b = lanes(half, width)
                    grad_ref[to, :] = jnp.where(first, a, b)
                    mom[to, :] = jnp.where(first, b, a)
                    to = pl.ds(spot * right_rows, right_rows)
                    n = width // 4
                    a, b = (v.astype(f32) for v in lanes(half + width, n))
                    low, high = jnp.where(first, a, b), jnp.where(first, b, a)
                    for part in range(2):
                        of = slice(part * right_rows, (part + 1) * right_rows)
                        right[to, part * n : (part + 1) * n] = low[of]
                        right[to, (2 + part) * n : (3 + part) * n] = high[of]
                    a, b = lanes(half + width + n, 2 * n)
                    both = GRAM_DECAY * (a.astype(f32) + b.astype(f32))
                    for part in range(2):
                        of = slice(part * right_rows, (part + 1) * right_rows)
                        rgram[to, part * 2 * n : (part + 1) * 2 * n] = both[of]
                    spot += 1
    basis, grad = basis_ref[...], grad_ref[...]
    rbasis = right[...].astype(bf16)

    n = second_rows_ref.shape[0]
    q = lax.broadcasted_iota(jnp.int32, (1, n), 1)
    r, far, q = q % share, (q // share) % NF, q // (share * NF)
    xhi, xlo, y, z = q % NXF, (q // NXF) % NXN, (q // NX) % NY, q // (NX * NY)
    wanted = (((z * NF + far) * NY + y) * NX + xhi * NXN + xlo) * rows + group * share + r
    column = (lax.broadcasted_iota(jnp.int32, (deep, n), 0) + core * half) % deep
    pick = jnp.where(column == wanted, 1.0, 0.0).astype(bf16)
    q = lax.broadcasted_iota(jnp.int32, (1, n), 1)
    own = jnp.where((column == row_first + q) & (q < rows), 1.0, 0.0).astype(bf16)
    columns = mm(basis, pick, 1, 0).astype(bf16)
    own_columns = mm(basis, own, 1, 0).astype(bf16)
    rotated_grad = mm(mm(columns, grad, 0, 0).astype(bf16), rbasis, 1, 0)
    rotated_moment = mm(mm(columns, mom[...], 0, 0).astype(bf16), rbasis, 1, 0)
    own_grad = mm(mm(own_columns, grad, 0, 0).astype(bf16), rbasis, 1, 0)[:rows]
    second_part = BETA_TWO * second_rows_ref[...] + (1.0 - BETA_TWO) * rotated_grad * rotated_grad
    second_new_ref[...] = BETA_TWO * second_ref[...] + (1.0 - BETA_TWO) * own_grad * own_grad
    direction = (rotated_moment / (jnp.sqrt(second_part) + ADAM_EPS)).astype(bf16)
    returned = mm(direction, rbasis, 1, 1).astype(bf16)
    own_rows = left_rows_ref[...]
    own_rows = jnp.where(first, own_rows, jnp.concatenate([own_rows[:, half:], own_rows[:, :half]], axis=1))
    update_ref[...] = mm(mm(own_rows, pick, 1, 0).astype(bf16), returned, 1, 0)

    own_grad = grad_ref[pl.ds(pl.multiple_of(row_first, rows), rows), :]
    left_new_ref[...] = GRAM_DECAY * left_gram_ref[...] + (1.0 - GRAM_DECAY) * mm(own_grad, grad, 1, 1)
    q = lax.broadcasted_iota(jnp.int32, (width, BLOCK), 1)
    column = lax.broadcasted_iota(jnp.int32, (width, BLOCK), 0)
    own = jnp.where((column == right_first + q) & (q < rows), 1.0, 0.0).astype(bf16)
    right_term_ref[...] = mm(mm(grad, own, 1, 0).astype(bf16), grad, 0, 0)[:rows]

    tile = 256

    def power_tile(t):
        at = pl.ds(t * tile, tile)
        whole = rgram[at, :] + (1.0 - GRAM_DECAY) * mm(grad_ref[:, t * tile : (t + 1) * tile], grad, 0, 0)
        high, low = split(whole)
        return mm(high, rbasis, 1, 0) + mm(low, rbasis, 1, 0)

    refresh(power_tile, width // tile, tile, right_first, rows, power, start, current, right_out_ref)


def mid_call(at, mine, other, second_rows, second, left_rows, left_gram):
    rows, deep = left_rows.shape
    width = second.shape[1]
    vmem = pl.BlockSpec(memory_space=pltpu.VMEM)
    shapes = [
        ((deep, deep), bf16), ((deep, width), bf16), ((rows, width), f32), ((rows, width), f32),
        ((rows, deep), f32), ((rows, width), f32), ((rows, width), f32),
    ]
    return pl.pallas_call(
        mid_kernel,
        out_shape=[jax.ShapeDtypeStruct(*v) for v in shapes],
        in_specs=[pl.BlockSpec(memory_space=pltpu.SMEM)] + [vmem] * 6,
        out_specs=[vmem] * len(shapes),
        scratch_shapes=[
            pltpu.VMEM((deep, width), bf16),
            pltpu.VMEM((width, width), f32),
            pltpu.VMEM((width, width), f32),
            pltpu.VMEM((width, width), f32),
            pltpu.VMEM((width, width), bf16),
            pltpu.VMEM((width, width), bf16),
        ],
        compiler_params=pltpu.CompilerParams(vmem_limit_bytes=40 << 20),
        cost_estimate=pl.CostEstimate(flops=6 * deep**3, transcendentals=width**2, bytes_accessed=12 * deep**2),
        name="middle",
    )(at, mine, other, second_rows, second, left_rows, left_gram)


def local(gradients, weight, moment, second, left_gram, left_basis, right_gram, right_basis):
    n_grp = CUT[0] * CUT[1]
    rows, width = weight.shape
    right_rows = right_gram.shape[0]
    n_shard = NZ * NF * NY * NX
    deep = n_shard * rows
    core = lax.axis_index("core")
    cube = (lax.axis_index("zhi") + CUT[0] - core * (1 - lax.axis_index("zlo"))) % CUT[0]
    group = cube * CUT[1] + core
    shard = lax.axis_index(SHARD)
    row_first = shard * rows
    right_first = shard * right_rows
    first = core == 0

    gradient = jnp.sum(gather(gradients[0], GRP, n_grp), axis=0) / n_grp
    moment_new = BETA_ONE * moment + (1.0 - BETA_ONE) * gradient
    grad_half = gradient.astype(bf16)
    moment_half = moment_new.astype(bf16)
    left_half = left_basis.astype(bf16)
    right_half = right_basis.astype(bf16)

    def fold(value, parts):
        return jnp.concatenate(jnp.split(value, parts, axis=1), axis=0)

    share = rows // n_grp
    own_second = jnp.concatenate([fold(v, 4) for v in pair(lax.dynamic_slice_in_dim(second, group * share, share, 0))], axis=0)
    start = (shard // (n_shard // BLOCKS)) * BLOCK
    round_gram = jnp.concatenate([left_gram, left_gram[:, : (SENT - 1) * BLOCK]], axis=1)
    sent_gram = lax.dynamic_slice_in_dim(round_gram, start, SENT * BLOCK, 1)
    half = deep // 2
    payload = jnp.concatenate(
        [
            jnp.where(first, left_half[:, :half], left_half[:, half:]),
            jnp.where(first, grad_half, moment_half),
            fold(jnp.where(first, right_half[:, : width // 2], right_half[:, width // 2 :]), 2),
            fold(jnp.where(first, *pair(right_gram)), 2),
            own_second,
            jnp.where(first, *pair(sent_gram)),
        ],
        axis=1,
    )
    cut = payload.shape[1] - SENT * BLOCK
    payload = gather(gather(payload, "yhi", NF), "xhi", NXF)
    near, groups = NZ * NY * NXN, cubes()
    parted = lambda v: v.reshape(NEAR + v.shape[1:])
    swap = [(0, 1), (1, 0)]
    early = gather(payload[..., :cut], AXES, near, groups)
    early_other = lax.ppermute(early, "core", swap)
    late = gather(payload[..., cut:], AXES, near, groups)

    second_parts = early[..., cut - 128 :].astype(f32)
    second_parts = second_parts[..., : rows // 2, :] + second_parts[..., rows // 2 :, :]
    second_rows = jnp.concatenate(jnp.split(second_parts, 4, axis=-2), axis=-1).reshape(-1, width)

    at = jnp.stack([core, group, row_first, right_first // rows * rows]).astype(jnp.int32)
    results = mid_call(at, parted(early), parted(early_other), second_rows, second, left_half, left_gram)
    results, late = lax.optimization_barrier((results, late))
    basis, grad, update, second_new, left_new, right_term, right_result = results
    late_other = lax.ppermute(late, "core", swap)
    updates = gather(update, GRP, n_grp)
    own = lambda v: lax.dynamic_slice_in_dim(v, right_first % rows, right_rows, 0)
    right_new = GRAM_DECAY * right_gram + (1.0 - GRAM_DECAY) * own(right_term)
    right_result = own(right_result)
    left_result = left_call(row_first[None], parted(late), parted(late_other), grad, basis, rows)
    updates, left_result = lax.optimization_barrier((updates, left_result))
    weight_new = weight - STEP_SIZE * jnp.sum(updates, axis=0)
    swapped = jnp.concatenate([left_result[:, half:], left_result[:, :half]], axis=1)
    left_result = jnp.where(first, left_result, swapped)
    return (weight_new, moment_new, second_new, left_new, left_result, right_new, right_result)


def solution(mesh):
    cut = Mesh(mesh.devices.reshape(CUT), AXES)
    rowwise = P(SHARD, None)
    return jax.shard_map(
        local,
        mesh=cut,
        in_specs=(P(GRP, SHARD, None),) + (rowwise,) * 7,
        out_specs=(rowwise,) * 7,
        check_vma=False,
    )
```

```python
import itertools

import jax
import jax.numpy as jnp
import numpy as np
from jax import lax
from jax.experimental import pallas as pl
from jax.experimental.pallas import tpu as pltpu
from jax.sharding import Mesh, PartitionSpec as P

NS_ITERS = 2

BETA_ONE = 0.9
BETA_TWO = 0.95
GRAM_DECAY = 0.95
ADAM_EPS = 1e-08
NORM_EPS = 1e-06
STEP_SIZE = 0.02
START_SCALE = 0.75

AXES = ("zhi", "core", "zlo", "yhi", "ylo", "xhi", "xlo")
CUT = (4, 2, 2, 4, 2, 2, 2)
GRP = ("zhi", "core")
SHARD = ("zlo", "yhi", "ylo", "xhi", "xlo")
NZ, NF, NY, NXF, NXN = CUT[2:]
NX = NXF * NXN
NEAR = (NZ, NY, NXN)
bf16 = jnp.bfloat16
f32 = jnp.float32

BLOCK = 128
BLOCKS = 8
SENT = BLOCKS // 2 + 1


def mm(a, b, ca, cb):
    return lax.dot_general(a, b, (((ca,), (cb,)), ((), ())), preferred_element_type=f32)


def cubes():
    groups = []
    deep, high, wide = CUT[0] * NZ, NF * NY, NX
    for core in range(CUT[1]):
        for corner in itertools.product(range(0, deep, 2), range(0, high, 2), range(0, wide, 2)):
            group = {}
            for step in itertools.product(range(2), repeat=3):
                z, y, x = (
                    (a + core + b) % n for a, b, n in zip(corner, step, (deep, high, wide))
                )
                place = (z // NZ, core, z % NZ, y // NY, y % NY, x // NXN, x % NXN)
                group[z % NZ, y % NY, x % NXN] = int(np.ravel_multi_index(place, CUT))
            groups.append([group[k] for k in sorted(group)])
    return groups


def gather(value, axes, size, groups=None):
    copies = jnp.broadcast_to(value[None], (size,) + value.shape)
    return lax.all_to_all(copies, axes, 0, 0, axis_index_groups=groups)


def pair(value):
    high = lax.reduce_precision(value, 8, 7)
    return high.astype(bf16), (value - high).astype(bf16)


def split(value):
    high = value.astype(bf16)
    return high, (value - high.astype(f32)).astype(bf16)


def refresh(power_tile, n_tiles, tile, first, count, power, start, current, out_ref):
    sums = None
    for t in range(n_tiles):
        p = power_tile(t)
        power[pl.ds(t * tile, tile), :] = p
        s = jnp.sum(p * p, axis=0, keepdims=True)
        sums = s if sums is None else sums + s
    scale = START_SCALE / jnp.sqrt(sums + NORM_EPS)
    for t in range(n_tiles):
        at = pl.ds(t * tile, tile)
        start[at, :] = (power[at, :] * scale).astype(bf16)
    x = start[...]
    for t in range(n_tiles):
        at = pl.ds(t * tile, tile)
        mine = start[at, :]
        square = mm(mine, x, 1, 1).astype(bf16)
        current[at, :] = (1.5 * mine.astype(f32) - 0.5 * mm(square, x, 1, 0)).astype(bf16)
    x = current[...]
    rows = current[pl.ds(pl.multiple_of(first, count), count), :]
    square = mm(rows, x, 1, 1).astype(bf16)
    out_ref[...] = 1.5 * rows.astype(f32) - 0.5 * mm(square, x, 1, 0)


def left_kernel(first_ref, mine_ref, other_ref, grad_ref, basis_ref, out_ref, gram, power, start, current):
    rows = mine_ref.shape[-2]
    for r in range(BLOCKS):
        zlo, far = r // NF, r % NF
        for j in range(SENT):
            c = (r + j) % BLOCKS
            at = pl.ds(j * BLOCK, BLOCK)
            pieces = []
            for near in range(NY * NX):
                y, x = near // NX, near % NX
                place = (zlo, y, x % NXN, x // NXN, far, slice(None), at)
                pieces.append(mine_ref[place].astype(f32) + other_ref[place].astype(f32))
            block = GRAM_DECAY * jnp.concatenate(pieces, axis=0)
            gram[r * BLOCK : (r + 1) * BLOCK, c * BLOCK : (c + 1) * BLOCK] = block
            if 0 < j < BLOCKS // 2:
                gram[c * BLOCK : (c + 1) * BLOCK, r * BLOCK : (r + 1) * BLOCK] = block.T
    grad = grad_ref[...]
    basis = basis_ref[...]
    tile = 256

    def power_tile(t):
        at = pl.ds(t * tile, tile)
        whole = gram[at, :] + (1.0 - GRAM_DECAY) * mm(grad_ref[at, :], grad, 1, 1)
        high, low = split(whole)
        return mm(high, basis, 1, 0) + mm(low, basis, 1, 0)

    refresh(power_tile, gram.shape[0] // tile, tile, first_ref[0], rows, power, start, current, out_ref)
    result, half = out_ref[...], gram.shape[0] // 2
    out_ref[...] = jnp.where(first_ref[1] == 0, result, jnp.concatenate([result[:, half:], result[:, :half]], axis=1))


def left_call(first, mine, other, grad, basis, rows):
    deep = basis.shape[0]
    vmem = pl.BlockSpec(memory_space=pltpu.VMEM)
    return pl.pallas_call(
        left_kernel,
        out_shape=jax.ShapeDtypeStruct((rows, deep), f32),
        in_specs=[pl.BlockSpec(memory_space=pltpu.SMEM)] + [vmem] * 4,
        out_specs=vmem,
        scratch_shapes=[
            pltpu.VMEM((deep, deep), f32),
            pltpu.VMEM((deep, deep), f32),
            pltpu.VMEM((deep, deep), bf16),
            pltpu.VMEM((deep, deep), bf16),
        ],
        compiler_params=pltpu.CompilerParams(vmem_limit_bytes=20 << 20),
        cost_estimate=pl.CostEstimate(flops=10 * deep**3, transcendentals=deep, bytes_accessed=8 * deep**2),
        name="left_refresh",
    )(first, mine, other, grad, basis)


def mid_kernel(
    at_ref, mine_ref, other_ref, second_ref, left_rows_ref, left_gram_ref, right_gram_ref,
    basis_ref, grad_ref, update_ref, second_new_ref, left_new_ref, right_new_ref, right_out_ref,
    mom, right, rgram, second_rows, term, power, start, current,
):
    right_pair, right_odd, group, row_first, core = (at_ref[i] for i in range(5))
    first = core == 0
    rows, width = second_ref.shape
    deep = basis_ref.shape[0]
    half = deep // 2
    share = second_rows.shape[0] // (deep // rows)
    right_rows = rows // 2
    spot = 0
    for zlo in range(NZ):
        for far in range(NF):
            for y in range(NY):
                for x in range(NX):
                    def lanes(at, n):
                        place = (zlo, y, x % NXN, x // NXN, far, slice(None), pl.ds(at, n))
                        return mine_ref[place], other_ref[place]

                    to = pl.ds(spot * rows, rows)
                    a, b = lanes(0, half)
                    basis_ref[to, :half] = a
                    basis_ref[to, half:] = b
                    a, b = lanes(half, width)
                    grad_ref[to, :] = jnp.where(first, a, b)
                    mom[to, :] = jnp.where(first, b, a)
                    to = pl.ds(spot * right_rows, right_rows)
                    n = width // 4
                    a, b = (v.astype(f32) for v in lanes(half + width, n))
                    low, high = jnp.where(first, a, b), jnp.where(first, b, a)
                    for part in range(2):
                        of = slice(part * right_rows, (part + 1) * right_rows)
                        right[to, part * n : (part + 1) * n] = low[of]
                        right[to, (2 + part) * n : (3 + part) * n] = high[of]
                    a, b = lanes(half + width + n, 2 * n)
                    both = GRAM_DECAY * (a.astype(f32) + b.astype(f32))
                    for part in range(2):
                        of = slice(part * right_rows, (part + 1) * right_rows)
                        rgram[to, part * 2 * n : (part + 1) * 2 * n] = both[of]
                    a, _ = lanes(half + width + 3 * n, n)
                    a = a.astype(f32)
                    both = a[:right_rows] + a[right_rows:]
                    for part in range(4):
                        of = slice(part * share, (part + 1) * share)
                        second_rows[spot * share : (spot + 1) * share, part * n : (part + 1) * n] = both[of]
                    spot += 1
    basis, grad = basis_ref[...], grad_ref[...]
    rbasis = right[...].astype(bf16)

    n = second_rows.shape[0]
    q = lax.broadcasted_iota(jnp.int32, (1, n), 1)
    wanted = q // share * rows + group * share + q % share
    column = (lax.broadcasted_iota(jnp.int32, (deep, n), 0) + core * half) % deep
    pick = jnp.where(column == wanted, 1.0, 0.0).astype(bf16)
    q = lax.broadcasted_iota(jnp.int32, (1, n), 1)
    own = jnp.where((column == row_first + q) & (q < rows), 1.0, 0.0).astype(bf16)
    columns = mm(basis, pick, 1, 0).astype(bf16)
    own_columns = mm(basis, own, 1, 0).astype(bf16)
    rotated_grad = mm(mm(columns, grad, 0, 0).astype(bf16), rbasis, 1, 0)
    rotated_moment = mm(mm(columns, mom[...], 0, 0).astype(bf16), rbasis, 1, 0)
    own_grad = mm(mm(own_columns, grad, 0, 0).astype(bf16), rbasis, 1, 0)[:rows]
    second_part = BETA_TWO * second_rows[...] + (1.0 - BETA_TWO) * rotated_grad * rotated_grad
    second_new_ref[...] = BETA_TWO * second_ref[...] + (1.0 - BETA_TWO) * own_grad * own_grad
    direction = (rotated_moment / (jnp.sqrt(second_part) + ADAM_EPS)).astype(bf16)
    returned = mm(direction, rbasis, 1, 1).astype(bf16)
    own_rows = left_rows_ref[...]
    own_rows = jnp.where(first, own_rows, jnp.concatenate([own_rows[:, half:], own_rows[:, :half]], axis=1))
    update_ref[...] = mm(mm(own_rows, pick, 1, 0).astype(bf16), returned, 1, 0)

    own_grad = grad_ref[pl.ds(pl.multiple_of(row_first, rows), rows), :]
    left_new_ref[...] = GRAM_DECAY * left_gram_ref[...] + (1.0 - GRAM_DECAY) * mm(own_grad, grad, 1, 1)
    q = lax.broadcasted_iota(jnp.int32, (width, BLOCK), 1)
    column = lax.broadcasted_iota(jnp.int32, (width, BLOCK), 0)
    own = jnp.where((column == right_pair + right_odd + q) & (q < right_rows), 1.0, 0.0).astype(bf16)
    own = mm(mm(grad, own, 1, 0).astype(bf16), grad, 0, 0)[:right_rows]
    right_new_ref[...] = GRAM_DECAY * right_gram_ref[...] + (1.0 - GRAM_DECAY) * own

    tile = 256

    def power_tile(t):
        at = pl.ds(t * tile, tile)
        whole = rgram[at, :] + (1.0 - GRAM_DECAY) * mm(grad_ref[:, t * tile : (t + 1) * tile], grad, 0, 0)
        high, low = split(whole)
        return mm(high, rbasis, 1, 0) + mm(low, rbasis, 1, 0)

    refresh(power_tile, width // tile, tile, right_pair, rows, power, start, current, term)
    right_out_ref[...] = term[pl.ds(pl.multiple_of(right_odd, right_rows), right_rows), :]


def mid_call(at, mine, other, second, left_rows, left_gram, right_gram):
    rows, deep = left_rows.shape
    width = second.shape[1]
    vmem = pl.BlockSpec(memory_space=pltpu.VMEM)
    shapes = [
        ((deep, deep), bf16), ((deep, width), bf16), ((rows, width), f32), ((rows, width), f32),
        ((rows, deep), f32), (right_gram.shape, f32), (right_gram.shape, f32),
    ]
    return pl.pallas_call(
        mid_kernel,
        out_shape=[jax.ShapeDtypeStruct(*v) for v in shapes],
        in_specs=[pl.BlockSpec(memory_space=pltpu.SMEM)] + [vmem] * 6,
        out_specs=[vmem] * len(shapes),
        scratch_shapes=[
            pltpu.VMEM((deep, width), bf16),
            pltpu.VMEM((width, width), f32),
            pltpu.VMEM((width, width), f32),
            pltpu.VMEM((deep // (CUT[0] * CUT[1]), width), f32),
            pltpu.VMEM((rows, width), f32),
            pltpu.VMEM((width, width), f32),
            pltpu.VMEM((width, width), bf16),
            pltpu.VMEM((width, width), bf16),
        ],
        compiler_params=pltpu.CompilerParams(vmem_limit_bytes=20 << 20),
        cost_estimate=pl.CostEstimate(flops=6 * deep**3, transcendentals=width**2, bytes_accessed=12 * deep**2),
        name="middle",
    )(at, mine, other, second, left_rows, left_gram, right_gram)


def local(gradients, weight, moment, second, left_gram, left_basis, right_gram, right_basis):
    n_grp = CUT[0] * CUT[1]
    rows, width = weight.shape
    right_rows = right_gram.shape[0]
    n_shard = NZ * NF * NY * NX
    deep = n_shard * rows
    core = lax.axis_index("core")
    cube = (lax.axis_index("zhi") + CUT[0] - core * (1 - lax.axis_index("zlo"))) % CUT[0]
    group = cube * CUT[1] + core
    shard = lax.axis_index(SHARD)
    row_first = shard * rows
    right_first = shard * right_rows
    first = core == 0

    gradient = jnp.sum(gather(gradients[0], GRP, n_grp), axis=0) / n_grp
    moment_new = BETA_ONE * moment + (1.0 - BETA_ONE) * gradient
    grad_half = gradient.astype(bf16)
    moment_half = moment_new.astype(bf16)
    left_half = left_basis.astype(bf16)
    right_half = right_basis.astype(bf16)

    def fold(value, parts):
        return jnp.concatenate(jnp.split(value, parts, axis=1), axis=0)

    share = rows // n_grp
    own_second = jnp.concatenate([fold(v, 4) for v in pair(lax.dynamic_slice_in_dim(second, group * share, share, 0))], axis=0)
    start = (shard // (n_shard // BLOCKS)) * BLOCK
    round_gram = jnp.concatenate([left_gram, left_gram[:, : (SENT - 1) * BLOCK]], axis=1)
    sent_gram = lax.dynamic_slice_in_dim(round_gram, start, SENT * BLOCK, 1)
    half = deep // 2
    payload = jnp.concatenate(
        [
            jnp.where(first, left_half[:, :half], left_half[:, half:]),
            jnp.where(first, grad_half, moment_half),
            fold(jnp.where(first, right_half[:, : width // 2], right_half[:, width // 2 :]), 2),
            fold(jnp.where(first, *pair(right_gram)), 2),
            own_second,
            jnp.where(first, *pair(sent_gram)),
        ],
        axis=1,
    )
    cut = payload.shape[1] - SENT * BLOCK
    payload = gather(payload, ("xhi", "yhi"), NXF * NF)
    payload = payload.reshape((NXF, NF) + payload.shape[1:])
    near, groups = NZ * NY * NXN, cubes()
    parted = lambda v: v.reshape(NEAR + v.shape[1:])
    swap = [(0, 1), (1, 0)]
    early = gather(payload[..., :cut], AXES, near, groups)
    early_other = lax.ppermute(early, "core", swap)
    late = gather(payload[..., cut:], AXES, near, groups)

    right_pair = right_first // rows * rows
    at = jnp.stack([right_pair, right_first - right_pair, group, row_first, core]).astype(jnp.int32)
    results = mid_call(at, parted(early), parted(early_other), second, left_half, left_gram, right_gram)
    basis, grad, update, second_new, left_new, right_new, right_result = results
    update, late = lax.optimization_barrier((update, late))
    late_other = lax.ppermute(late, "core", swap)
    updates = gather(update, GRP, n_grp)
    left_result = left_call(at[3:], parted(late), parted(late_other), grad, basis, rows)
    updates, left_result = lax.optimization_barrier((updates, left_result))
    weight_new = weight - STEP_SIZE * jnp.sum(updates, axis=0)
    return (weight_new, moment_new, second_new, left_new, left_result, right_new, right_result)


def solution(mesh):
    cut = Mesh(mesh.devices.reshape(CUT), AXES)
    rowwise = P(SHARD, None)
    return jax.shard_map(
        local,
        mesh=cut,
        in_specs=(P(GRP, SHARD, None),) + (rowwise,) * 7,
        out_specs=(rowwise,) * 7,
        check_vma=False,
    )
```

```python
import itertools

import jax
import jax.numpy as jnp
import numpy as np
from jax import lax
from jax.experimental import pallas as pl
from jax.experimental.pallas import tpu as pltpu
from jax.sharding import Mesh, PartitionSpec as P

NS_ITERS = 2

BETA_ONE = 0.9
BETA_TWO = 0.95
GRAM_DECAY = 0.95
ADAM_EPS = 1e-08
NORM_EPS = 1e-06
STEP_SIZE = 0.02
START_SCALE = 0.75

AXES = ("zhi", "core", "zlo", "yhi", "ylo", "xhi", "xlo")
CUT = (4, 2, 2, 4, 2, 2, 2)
GRP = ("zhi", "core")
SHARD = ("zlo", "yhi", "ylo", "xhi", "xlo")
NZ, NF, NY, NXF, NXN = CUT[2:]
NX = NXF * NXN
NEAR = (NZ, NY, NXN)
bf16 = jnp.bfloat16
f32 = jnp.float32

BLOCK = 128
BLOCKS = 8
SENT = BLOCKS // 2 + 1


def mm(a, b, ca, cb):
    return lax.dot_general(a, b, (((ca,), (cb,)), ((), ())), preferred_element_type=f32)


def cubes():
    groups = []
    deep, high, wide = CUT[0] * NZ, NF * NY, NX
    for core in range(CUT[1]):
        for corner in itertools.product(range(0, deep, 2), range(0, high, 2), range(0, wide, 2)):
            group = {}
            for step in itertools.product(range(2), repeat=3):
                z, y, x = (
                    (a + core + b) % n for a, b, n in zip(corner, step, (deep, high, wide))
                )
                place = (z // NZ, core, z % NZ, y // NY, y % NY, x // NXN, x % NXN)
                group[z % NZ, y % NY, x % NXN] = int(np.ravel_multi_index(place, CUT))
            groups.append([group[k] for k in sorted(group)])
    return groups


def gather(value, axes, size, groups=None):
    copies = jnp.broadcast_to(value[None], (size,) + value.shape)
    return lax.all_to_all(copies, axes, 0, 0, axis_index_groups=groups)


def pair(value):
    high = lax.reduce_precision(value, 8, 7)
    return high.astype(bf16), (value - high).astype(bf16)


def split(value):
    high = value.astype(bf16)
    return high, (value - high.astype(f32)).astype(bf16)


def refresh(power_tile, n_tiles, tile, first, count, power, start, current, out_ref):
    sums = None
    for t in range(n_tiles):
        p = power_tile(t)
        power[pl.ds(t * tile, tile), :] = p
        s = jnp.sum(p * p, axis=0, keepdims=True)
        sums = s if sums is None else sums + s
    scale = START_SCALE / jnp.sqrt(sums + NORM_EPS)
    for t in range(n_tiles):
        at = pl.ds(t * tile, tile)
        start[at, :] = (power[at, :] * scale).astype(bf16)
    x = start[...]
    for t in range(n_tiles):
        at = pl.ds(t * tile, tile)
        mine = start[at, :]
        square = mm(mine, x, 1, 1).astype(bf16)
        current[at, :] = (1.5 * mine.astype(f32) - 0.5 * mm(square, x, 1, 0)).astype(bf16)
    x = current[...]
    rows = current[pl.ds(pl.multiple_of(first, count), count), :]
    square = mm(rows, x, 1, 1).astype(bf16)
    out_ref[...] = 1.5 * rows.astype(f32) - 0.5 * mm(square, x, 1, 0)


def left_kernel(
    first_ref, mine_hbm, other_hbm, grad_hbm, basis_hbm, out_ref,
    mine_ref, other_ref, grad_ref, basis_ref, gram, power, start, current, sems,
):
    pairs = ((grad_hbm, grad_ref), (mine_hbm, mine_ref), (other_hbm, other_ref), (basis_hbm, basis_ref))
    copies = [pltpu.make_async_copy(a, b, sems.at[i]) for i, (a, b) in enumerate(pairs)]
    for copy in copies:
        copy.start()
    rows, deep = mine_ref.shape[-2], basis_ref.shape[0]
    tile = 256
    copies[0].wait()
    grad = grad_ref[...]
    for t in range(deep // tile):
        at = pl.ds(t * tile, tile)
        power[at, :] = (1.0 - GRAM_DECAY) * mm(grad_ref[at, :], grad, 1, 1)
    copies[1].wait()
    copies[2].wait()
    for r in range(BLOCKS):
        zlo, far = r // NF, r % NF
        for j in range(SENT):
            c = (r + j) % BLOCKS
            at = pl.ds(j * BLOCK, BLOCK)
            pieces = []
            for near in range(NY * NX):
                y, x = near // NX, near % NX
                place = (zlo, y, x % NXN, x // NXN, far, slice(None), at)
                pieces.append(mine_ref[place].astype(f32) + other_ref[place].astype(f32))
            block = GRAM_DECAY * jnp.concatenate(pieces, axis=0)
            gram[r * BLOCK : (r + 1) * BLOCK, c * BLOCK : (c + 1) * BLOCK] = block
            if 0 < j < BLOCKS // 2:
                gram[c * BLOCK : (c + 1) * BLOCK, r * BLOCK : (r + 1) * BLOCK] = block.T
    copies[3].wait()
    basis = basis_ref[...]

    def power_tile(t):
        at = pl.ds(t * tile, tile)
        high, low = split(gram[at, :] + power[at, :])
        return mm(high, basis, 1, 0) + mm(low, basis, 1, 0)

    refresh(power_tile, deep // tile, tile, first_ref[0], rows, power, start, current, out_ref)
    result, half = out_ref[...], deep // 2
    out_ref[...] = jnp.where(first_ref[1] == 0, result, jnp.concatenate([result[:, half:], result[:, :half]], axis=1))


def left_call(first, mine, other, grad, basis, rows):
    deep = basis.shape[0]
    hbm = pl.BlockSpec(memory_space=pltpu.HBM)
    anywhere = pl.BlockSpec(memory_space=pl.ANY)
    return pl.pallas_call(
        left_kernel,
        out_shape=jax.ShapeDtypeStruct((rows, deep), f32),
        in_specs=[pl.BlockSpec(memory_space=pltpu.SMEM), anywhere, anywhere, hbm, hbm],
        out_specs=pl.BlockSpec(memory_space=pltpu.VMEM),
        scratch_shapes=[pltpu.VMEM(v.shape, bf16) for v in (mine, other, grad, basis)]
        + [
            pltpu.VMEM((deep, deep), f32),
            pltpu.VMEM((deep, deep), f32),
            pltpu.VMEM((deep, deep), bf16),
            pltpu.VMEM((deep, deep), bf16),
            pltpu.SemaphoreType.DMA((4,)),
        ],
        compiler_params=pltpu.CompilerParams(vmem_limit_bytes=28 << 20),
        cost_estimate=pl.CostEstimate(flops=10 * deep**3, transcendentals=deep, bytes_accessed=8 * deep**2),
        name="left_refresh",
    )(first, mine, other, grad, basis)


def mid_kernel(
    at_ref, mine_ref, other_ref, second_ref, left_rows_ref, left_gram_ref, right_gram_ref,
    basis_hbm, grad_hbm, update_ref, second_new_ref, left_new_ref, right_new_ref, right_out_ref,
    basis_ref, grad_ref, sems, mom, right, rgram, second_rows, term, power, start, current,
):
    right_pair, right_odd, group, row_first, core = (at_ref[i] for i in range(5))
    first = core == 0
    rows, width = second_ref.shape
    deep = basis_ref.shape[0]
    half = deep // 2
    share = second_rows.shape[0] // (deep // rows)
    right_rows = rows // 2
    spot = 0
    for zlo in range(NZ):
        for far in range(NF):
            for y in range(NY):
                for x in range(NX):
                    def lanes(at, n):
                        place = (zlo, y, x % NXN, x // NXN, far, slice(None), pl.ds(at, n))
                        return mine_ref[place], other_ref[place]

                    to = pl.ds(spot * rows, rows)
                    a, b = lanes(0, half)
                    basis_ref[to, :half] = a
                    basis_ref[to, half:] = b
                    a, b = lanes(half, width)
                    grad_ref[to, :] = jnp.where(first, a, b)
                    mom[to, :] = jnp.where(first, b, a)
                    to = pl.ds(spot * right_rows, right_rows)
                    n = width // 4
                    a, b = (v.astype(f32) for v in lanes(half + width, n))
                    low, high = jnp.where(first, a, b), jnp.where(first, b, a)
                    for part in range(2):
                        of = slice(part * right_rows, (part + 1) * right_rows)
                        right[to, part * n : (part + 1) * n] = low[of]
                        right[to, (2 + part) * n : (3 + part) * n] = high[of]
                    a, b = lanes(half + width + n, 2 * n)
                    both = GRAM_DECAY * (a.astype(f32) + b.astype(f32))
                    for part in range(2):
                        of = slice(part * right_rows, (part + 1) * right_rows)
                        rgram[to, part * 2 * n : (part + 1) * 2 * n] = both[of]
                    a, _ = lanes(half + width + 3 * n, n)
                    a = a.astype(f32)
                    both = a[:right_rows] + a[right_rows:]
                    for part in range(4):
                        of = slice(part * share, (part + 1) * share)
                        second_rows[spot * share : (spot + 1) * share, part * n : (part + 1) * n] = both[of]
                    spot += 1
    copies = [
        pltpu.make_async_copy(basis_ref, basis_hbm, sems.at[0]),
        pltpu.make_async_copy(grad_ref, grad_hbm, sems.at[1]),
    ]
    for copy in copies:
        copy.start()
    basis, grad = basis_ref[...], grad_ref[...]
    rbasis = right[...].astype(bf16)

    n = second_rows.shape[0]
    q = lax.broadcasted_iota(jnp.int32, (1, n), 1)
    wanted = q // share * rows + group * share + q % share
    column = (lax.broadcasted_iota(jnp.int32, (deep, n), 0) + core * half) % deep
    pick = jnp.where(column == wanted, 1.0, 0.0).astype(bf16)
    q = lax.broadcasted_iota(jnp.int32, (1, n), 1)
    own = jnp.where((column == row_first + q) & (q < rows), 1.0, 0.0).astype(bf16)
    columns = mm(basis, pick, 1, 0).astype(bf16)
    own_columns = mm(basis, own, 1, 0).astype(bf16)
    rotated_grad = mm(mm(columns, grad, 0, 0).astype(bf16), rbasis, 1, 0)
    rotated_moment = mm(mm(columns, mom[...], 0, 0).astype(bf16), rbasis, 1, 0)
    own_grad = mm(mm(own_columns, grad, 0, 0).astype(bf16), rbasis, 1, 0)[:rows]
    second_part = BETA_TWO * second_rows[...] + (1.0 - BETA_TWO) * rotated_grad * rotated_grad
    second_new_ref[...] = BETA_TWO * second_ref[...] + (1.0 - BETA_TWO) * own_grad * own_grad
    direction = (rotated_moment / (jnp.sqrt(second_part) + ADAM_EPS)).astype(bf16)
    returned = mm(direction, rbasis, 1, 1).astype(bf16)
    own_rows = left_rows_ref[...]
    own_rows = jnp.where(first, own_rows, jnp.concatenate([own_rows[:, half:], own_rows[:, :half]], axis=1))
    update_ref[...] = mm(mm(own_rows, pick, 1, 0).astype(bf16), returned, 1, 0)

    own_grad = grad_ref[pl.ds(pl.multiple_of(row_first, rows), rows), :]
    left_new_ref[...] = GRAM_DECAY * left_gram_ref[...] + (1.0 - GRAM_DECAY) * mm(own_grad, grad, 1, 1)
    q = lax.broadcasted_iota(jnp.int32, (width, BLOCK), 1)
    column = lax.broadcasted_iota(jnp.int32, (width, BLOCK), 0)
    own = jnp.where((column == right_pair + right_odd + q) & (q < right_rows), 1.0, 0.0).astype(bf16)
    own = mm(mm(grad, own, 1, 0).astype(bf16), grad, 0, 0)[:right_rows]
    right_new_ref[...] = GRAM_DECAY * right_gram_ref[...] + (1.0 - GRAM_DECAY) * own

    tile = 256

    def power_tile(t):
        at = pl.ds(t * tile, tile)
        whole = rgram[at, :] + (1.0 - GRAM_DECAY) * mm(grad_ref[:, t * tile : (t + 1) * tile], grad, 0, 0)
        high, low = split(whole)
        return mm(high, rbasis, 1, 0) + mm(low, rbasis, 1, 0)

    refresh(power_tile, width // tile, tile, right_pair, rows, power, start, current, term)
    right_out_ref[...] = term[pl.ds(pl.multiple_of(right_odd, right_rows), right_rows), :]
    for copy in copies:
        copy.wait()


def mid_call(at, mine, other, second, left_rows, left_gram, right_gram):
    rows, deep = left_rows.shape
    width = second.shape[1]
    vmem = pl.BlockSpec(memory_space=pltpu.VMEM)
    shapes = [
        ((deep, deep), bf16), ((deep, width), bf16), ((rows, width), f32), ((rows, width), f32),
        ((rows, deep), f32), (right_gram.shape, f32), (right_gram.shape, f32),
    ]
    return pl.pallas_call(
        mid_kernel,
        out_shape=[pltpu.HBM(*v) for v in shapes[:2]] + [jax.ShapeDtypeStruct(*v) for v in shapes[2:]],
        in_specs=[pl.BlockSpec(memory_space=pltpu.SMEM)] + [vmem] * 6,
        out_specs=[pl.BlockSpec(memory_space=pltpu.HBM)] * 2 + [vmem] * (len(shapes) - 2),
        scratch_shapes=[
            pltpu.VMEM((deep, deep), bf16),
            pltpu.VMEM((deep, width), bf16),
            pltpu.SemaphoreType.DMA((2,)),
            pltpu.VMEM((deep, width), bf16),
            pltpu.VMEM((width, width), f32),
            pltpu.VMEM((width, width), f32),
            pltpu.VMEM((deep // (CUT[0] * CUT[1]), width), f32),
            pltpu.VMEM((rows, width), f32),
            pltpu.VMEM((width, width), f32),
            pltpu.VMEM((width, width), bf16),
            pltpu.VMEM((width, width), bf16),
        ],
        compiler_params=pltpu.CompilerParams(vmem_limit_bytes=20 << 20),
        cost_estimate=pl.CostEstimate(flops=6 * deep**3, transcendentals=width**2, bytes_accessed=12 * deep**2),
        name="middle",
    )(at, mine, other, second, left_rows, left_gram, right_gram)


def local(gradients, weight, moment, second, left_gram, left_basis, right_gram, right_basis):
    n_grp = CUT[0] * CUT[1]
    rows, width = weight.shape
    right_rows = right_gram.shape[0]
    n_shard = NZ * NF * NY * NX
    deep = n_shard * rows
    core = lax.axis_index("core")
    cube = (lax.axis_index("zhi") + CUT[0] - core * (1 - lax.axis_index("zlo"))) % CUT[0]
    group = cube * CUT[1] + core
    shard = lax.axis_index(SHARD)
    row_first = shard * rows
    right_first = shard * right_rows
    first = core == 0

    gradient = jnp.sum(gather(gradients[0], GRP, n_grp), axis=0) / n_grp
    moment_new = BETA_ONE * moment + (1.0 - BETA_ONE) * gradient
    grad_half = gradient.astype(bf16)
    moment_half = moment_new.astype(bf16)
    left_half = left_basis.astype(bf16)
    right_half = right_basis.astype(bf16)

    def fold(value, parts):
        return jnp.concatenate(jnp.split(value, parts, axis=1), axis=0)

    share = rows // n_grp
    own_second = jnp.concatenate([fold(v, 4) for v in pair(lax.dynamic_slice_in_dim(second, group * share, share, 0))], axis=0)
    start = (shard // (n_shard // BLOCKS)) * BLOCK
    round_gram = jnp.concatenate([left_gram, left_gram[:, : (SENT - 1) * BLOCK]], axis=1)
    sent_gram = lax.dynamic_slice_in_dim(round_gram, start, SENT * BLOCK, 1)
    half = deep // 2
    payload = jnp.concatenate(
        [
            jnp.where(first, left_half[:, :half], left_half[:, half:]),
            jnp.where(first, grad_half, moment_half),
            fold(jnp.where(first, right_half[:, : width // 2], right_half[:, width // 2 :]), 2),
            fold(jnp.where(first, *pair(right_gram)), 2),
            own_second,
            jnp.where(first, *pair(sent_gram)),
        ],
        axis=1,
    )
    cut = payload.shape[1] - SENT * BLOCK
    payload = gather(payload, ("xhi", "yhi"), NXF * NF)
    payload = payload.reshape((NXF, NF) + payload.shape[1:])
    near, groups = NZ * NY * NXN, cubes()
    parted = lambda v: v.reshape(NEAR + v.shape[1:])
    swap = [(0, 1), (1, 0)]
    early = gather(payload[..., :cut], AXES, near, groups)
    early_other = lax.ppermute(early, "core", swap)
    late = gather(payload[..., cut:], AXES, near, groups)

    right_pair = right_first // rows * rows
    at = jnp.stack([right_pair, right_first - right_pair, group, row_first, core]).astype(jnp.int32)
    results = mid_call(at, parted(early), parted(early_other), second, left_half, left_gram, right_gram)
    basis, grad, update, second_new, left_new, right_new, right_result = results
    update, late = lax.optimization_barrier((update, late))
    late_other = lax.ppermute(late, "core", swap)
    updates = gather(update, GRP, n_grp)
    basis, grad = (pltpu.with_memory_space_constraint(v, pltpu.HBM) for v in (basis, grad))
    left_result = left_call(at[3:], parted(late), parted(late_other), grad, basis, rows)
    updates, left_result = lax.optimization_barrier((updates, left_result))
    weight_new = weight - STEP_SIZE * jnp.sum(updates, axis=0)
    return (weight_new, moment_new, second_new, left_new, left_result, right_new, right_result)


def solution(mesh):
    cut = Mesh(mesh.devices.reshape(CUT), AXES)
    rowwise = P(SHARD, None)
    return jax.shard_map(
        local,
        mesh=cut,
        in_specs=(P(GRP, SHARD, None),) + (rowwise,) * 7,
        out_specs=(rowwise,) * 7,
        check_vma=False,
    )
```

```python
import itertools

import jax
import jax.numpy as jnp
import numpy as np
from jax import lax
from jax.experimental import pallas as pl
from jax.experimental.pallas import tpu as pltpu
from jax.sharding import Mesh, PartitionSpec as P

NS_ITERS = 2

BETA_ONE = 0.9
BETA_TWO = 0.95
GRAM_DECAY = 0.95
ADAM_EPS = 1e-08
NORM_EPS = 1e-06
STEP_SIZE = 0.02
START_SCALE = 0.75

AXES = ("zhi", "core", "zlo", "yhi", "ylo", "xhi", "xlo")
CUT = (4, 2, 2, 4, 2, 2, 2)
GRP = ("zhi", "core")
SHARD = ("zlo", "yhi", "ylo", "xhi", "xlo")
NZ, NF, NY, NXF, NXN = CUT[2:]
NX = NXF * NXN
NEAR = (NZ, NY, NXN)
bf16 = jnp.bfloat16
f32 = jnp.float32

BLOCK = 128
BLOCKS = 8
SENT = BLOCKS // 2 + 1


def mm(a, b, ca, cb):
    return lax.dot_general(a, b, (((ca,), (cb,)), ((), ())), preferred_element_type=f32)


def cubes():
    groups = []
    deep, high, wide = CUT[0] * NZ, NF * NY, NX
    for core in range(CUT[1]):
        for corner in itertools.product(range(0, deep, 2), range(0, high, 2), range(0, wide, 2)):
            group = {}
            for step in itertools.product(range(2), repeat=3):
                z, y, x = (
                    (a + core + b) % n for a, b, n in zip(corner, step, (deep, high, wide))
                )
                place = (z // NZ, core, z % NZ, y // NY, y % NY, x // NXN, x % NXN)
                group[z % NZ, y % NY, x % NXN] = int(np.ravel_multi_index(place, CUT))
            groups.append([group[k] for k in sorted(group)])
    return groups


def gather(value, axes, size, groups=None):
    copies = jnp.broadcast_to(value[None], (size,) + value.shape)
    return lax.all_to_all(copies, axes, 0, 0, axis_index_groups=groups)


def pair(value):
    high = lax.reduce_precision(value, 8, 7)
    return high.astype(bf16), (value - high).astype(bf16)


def split(value):
    high = value.astype(bf16)
    return high, (value - high.astype(f32)).astype(bf16)


def refresh(power_tile, n_tiles, tile, first, count, power, start, current, out_ref):
    sums = None
    for t in range(n_tiles):
        p = power_tile(t)
        power[pl.ds(t * tile, tile), :] = p
        s = jnp.sum(p * p, axis=0, keepdims=True)
        sums = s if sums is None else sums + s
    scale = START_SCALE / jnp.sqrt(sums + NORM_EPS)
    for t in range(n_tiles):
        at = pl.ds(t * tile, tile)
        start[at, :] = (power[at, :] * scale).astype(bf16)
    x = start[...]
    for t in range(n_tiles):
        at = pl.ds(t * tile, tile)
        mine = start[at, :]
        square = mm(mine, x, 1, 1).astype(bf16)
        current[at, :] = (1.5 * mine.astype(f32) - 0.5 * mm(square, x, 1, 0)).astype(bf16)
    x = current[...]
    rows = current[pl.ds(pl.multiple_of(first, count), count), :]
    square = mm(rows, x, 1, 1).astype(bf16)
    out_ref[...] = 1.5 * rows.astype(f32) - 0.5 * mm(square, x, 1, 0)


def left_kernel(
    first_ref, mine_hbm, other_hbm, outer_hbm, basis_hbm, out_ref,
    mine_ref, other_ref, basis_ref, gram, power, start, current, sems,
):
    pairs = ((mine_hbm, mine_ref), (other_hbm, other_ref), (outer_hbm, power), (basis_hbm, basis_ref))
    copies = [pltpu.make_async_copy(a, b, sems.at[i]) for i, (a, b) in enumerate(pairs)]
    for copy in copies:
        copy.start()
    rows, deep, tile = mine_ref.shape[-2], basis_ref.shape[0], 256
    copies[0].wait()
    copies[1].wait()
    for r in range(BLOCKS):
        zlo, far = r // NF, r % NF
        for j in range(SENT):
            c = (r + j) % BLOCKS
            at = pl.ds(j * BLOCK, BLOCK)
            pieces = []
            for near in range(NY * NX):
                y, x = near // NX, near % NX
                place = (zlo, y, x % NXN, x // NXN, far, slice(None), at)
                pieces.append(mine_ref[place].astype(f32) + other_ref[place].astype(f32))
            block = GRAM_DECAY * jnp.concatenate(pieces, axis=0)
            gram[r * BLOCK : (r + 1) * BLOCK, c * BLOCK : (c + 1) * BLOCK] = block
            if 0 < j < BLOCKS // 2:
                gram[c * BLOCK : (c + 1) * BLOCK, r * BLOCK : (r + 1) * BLOCK] = block.T
    copies[2].wait()
    copies[3].wait()
    basis = basis_ref[...]

    def power_tile(t):
        at = pl.ds(t * tile, tile)
        high, low = split(gram[at, :] + power[at, :])
        return mm(high, basis, 1, 0) + mm(low, basis, 1, 0)

    refresh(power_tile, deep // tile, tile, first_ref[0], rows, power, start, current, out_ref)
    result, half = out_ref[...], deep // 2
    out_ref[...] = jnp.where(first_ref[1] == 0, result, jnp.concatenate([result[:, half:], result[:, :half]], axis=1))


def left_call(first, mine, other, outer, basis, rows):
    deep = basis.shape[0]
    hbm = pl.BlockSpec(memory_space=pltpu.HBM)
    anywhere = pl.BlockSpec(memory_space=pl.ANY)
    return pl.pallas_call(
        left_kernel,
        out_shape=jax.ShapeDtypeStruct((rows, deep), f32),
        in_specs=[pl.BlockSpec(memory_space=pltpu.SMEM), anywhere, anywhere, hbm, hbm],
        out_specs=pl.BlockSpec(memory_space=pltpu.VMEM),
        scratch_shapes=[pltpu.VMEM(v.shape, bf16) for v in (mine, other, basis)]
        + [
            pltpu.VMEM((deep, deep), f32),
            pltpu.VMEM((deep, deep), f32),
            pltpu.VMEM((deep, deep), bf16),
            pltpu.VMEM((deep, deep), bf16),
            pltpu.SemaphoreType.DMA((4,)),
        ],
        compiler_params=pltpu.CompilerParams(vmem_limit_bytes=28 << 20),
        cost_estimate=pl.CostEstimate(flops=10 * deep**3, transcendentals=deep, bytes_accessed=8 * deep**2),
        name="left_refresh",
    )(first, mine, other, outer, basis)


def mid_kernel(
    at_ref, mine_ref, other_ref, second_ref, left_rows_ref, left_gram_ref, right_gram_ref,
    basis_hbm, outer_hbm, update_ref, second_new_ref, left_new_ref, right_new_ref, right_out_ref,
    basis_ref, grad_ref, outer, sems, mom, right, rgram, second_rows, term, power, start, current,
):
    right_pair, right_odd, group, row_first, core = (at_ref[i] for i in range(5))
    first = core == 0
    rows, width = second_ref.shape
    deep = basis_ref.shape[0]
    half = deep // 2
    share = second_rows.shape[0] // (deep // rows)
    right_rows = rows // 2
    spot = 0
    for zlo in range(NZ):
        for far in range(NF):
            for y in range(NY):
                for x in range(NX):
                    def lanes(at, n):
                        place = (zlo, y, x % NXN, x // NXN, far, slice(None), pl.ds(at, n))
                        return mine_ref[place], other_ref[place]

                    to = pl.ds(spot * rows, rows)
                    a, b = lanes(0, half)
                    basis_ref[to, :half] = a
                    basis_ref[to, half:] = b
                    a, b = lanes(half, width)
                    grad_ref[to, :] = jnp.where(first, a, b)
                    mom[to, :] = jnp.where(first, b, a)
                    to = pl.ds(spot * right_rows, right_rows)
                    n = width // 4
                    a, b = (v.astype(f32) for v in lanes(half + width, n))
                    low, high = jnp.where(first, a, b), jnp.where(first, b, a)
                    for part in range(2):
                        of = slice(part * right_rows, (part + 1) * right_rows)
                        right[to, part * n : (part + 1) * n] = low[of]
                        right[to, (2 + part) * n : (3 + part) * n] = high[of]
                    a, b = lanes(half + width + n, 2 * n)
                    both = GRAM_DECAY * (a.astype(f32) + b.astype(f32))
                    for part in range(2):
                        of = slice(part * right_rows, (part + 1) * right_rows)
                        rgram[to, part * 2 * n : (part + 1) * 2 * n] = both[of]
                    a, _ = lanes(half + width + 3 * n, n)
                    a = a.astype(f32)
                    both = a[:right_rows] + a[right_rows:]
                    for part in range(4):
                        of = slice(part * share, (part + 1) * share)
                        second_rows[spot * share : (spot + 1) * share, part * n : (part + 1) * n] = both[of]
                    spot += 1
    copies = [
        pltpu.make_async_copy(basis_ref, basis_hbm, sems.at[0]),
        pltpu.make_async_copy(outer, outer_hbm, sems.at[1]),
    ]
    copies[0].start()
    basis, grad = basis_ref[...], grad_ref[...]
    tile = 256
    for t in range(deep // tile):
        to = pl.ds(t * tile, tile)
        outer[to, :] = (1.0 - GRAM_DECAY) * mm(grad_ref[to, :], grad, 1, 1)
    copies[1].start()
    rbasis = right[...].astype(bf16)

    n = second_rows.shape[0]
    q = lax.broadcasted_iota(jnp.int32, (1, n), 1)
    wanted = q // share * rows + group * share + q % share
    column = (lax.broadcasted_iota(jnp.int32, (deep, n), 0) + core * half) % deep
    pick = jnp.where(column == wanted, 1.0, 0.0).astype(bf16)
    q = lax.broadcasted_iota(jnp.int32, (1, n), 1)
    own = jnp.where((column == row_first + q) & (q < rows), 1.0, 0.0).astype(bf16)
    columns = mm(basis, pick, 1, 0).astype(bf16)
    own_columns = mm(basis, own, 1, 0).astype(bf16)
    rotated_grad = mm(mm(columns, grad, 0, 0).astype(bf16), rbasis, 1, 0)
    rotated_moment = mm(mm(columns, mom[...], 0, 0).astype(bf16), rbasis, 1, 0)
    own_grad = mm(mm(own_columns, grad, 0, 0).astype(bf16), rbasis, 1, 0)[:rows]
    second_part = BETA_TWO * second_rows[...] + (1.0 - BETA_TWO) * rotated_grad * rotated_grad
    second_new_ref[...] = BETA_TWO * second_ref[...] + (1.0 - BETA_TWO) * own_grad * own_grad
    direction = (rotated_moment / (jnp.sqrt(second_part) + ADAM_EPS)).astype(bf16)
    returned = mm(direction, rbasis, 1, 1).astype(bf16)
    own_rows = left_rows_ref[...]
    own_rows = jnp.where(first, own_rows, jnp.concatenate([own_rows[:, half:], own_rows[:, :half]], axis=1))
    update_ref[...] = mm(mm(own_rows, pick, 1, 0).astype(bf16), returned, 1, 0)

    own_at = pl.ds(pl.multiple_of(row_first, rows), rows)
    left_new_ref[...] = GRAM_DECAY * left_gram_ref[...] + outer[own_at, :]
    q = lax.broadcasted_iota(jnp.int32, (width, BLOCK), 1)
    column = lax.broadcasted_iota(jnp.int32, (width, BLOCK), 0)
    own = jnp.where((column == right_pair + right_odd + q) & (q < right_rows), 1.0, 0.0).astype(bf16)
    own = mm(mm(grad, own, 1, 0).astype(bf16), grad, 0, 0)[:right_rows]
    right_new_ref[...] = GRAM_DECAY * right_gram_ref[...] + (1.0 - GRAM_DECAY) * own

    def power_tile(t):
        at = pl.ds(t * tile, tile)
        whole = rgram[at, :] + (1.0 - GRAM_DECAY) * mm(grad_ref[:, t * tile : (t + 1) * tile], grad, 0, 0)
        high, low = split(whole)
        return mm(high, rbasis, 1, 0) + mm(low, rbasis, 1, 0)

    refresh(power_tile, width // tile, tile, right_pair, rows, power, start, current, term)
    right_out_ref[...] = term[pl.ds(pl.multiple_of(right_odd, right_rows), right_rows), :]
    for copy in copies:
        copy.wait()


def mid_call(at, mine, other, second, left_rows, left_gram, right_gram):
    rows, deep = left_rows.shape
    width = second.shape[1]
    vmem = pl.BlockSpec(memory_space=pltpu.VMEM)
    shapes = [
        ((deep, deep), bf16), ((deep, deep), f32), ((rows, width), f32), ((rows, width), f32),
        ((rows, deep), f32), (right_gram.shape, f32), (right_gram.shape, f32),
    ]
    return pl.pallas_call(
        mid_kernel,
        out_shape=[pltpu.HBM(*v) for v in shapes[:2]] + [jax.ShapeDtypeStruct(*v) for v in shapes[2:]],
        in_specs=[pl.BlockSpec(memory_space=pltpu.SMEM)] + [vmem] * 6,
        out_specs=[pl.BlockSpec(memory_space=pltpu.HBM)] * 2 + [vmem] * (len(shapes) - 2),
        scratch_shapes=[
            pltpu.VMEM((deep, deep), bf16),
            pltpu.VMEM((deep, width), bf16),
            pltpu.VMEM((deep, deep), f32),
            pltpu.SemaphoreType.DMA((2,)),
            pltpu.VMEM((deep, width), bf16),
            pltpu.VMEM((width, width), f32),
            pltpu.VMEM((width, width), f32),
            pltpu.VMEM((deep // (CUT[0] * CUT[1]), width), f32),
            pltpu.VMEM((rows, width), f32),
            pltpu.VMEM((width, width), f32),
            pltpu.VMEM((width, width), bf16),
            pltpu.VMEM((width, width), bf16),
        ],
        compiler_params=pltpu.CompilerParams(vmem_limit_bytes=24 << 20),
        cost_estimate=pl.CostEstimate(flops=6 * deep**3, transcendentals=width**2, bytes_accessed=12 * deep**2),
        name="middle",
    )(at, mine, other, second, left_rows, left_gram, right_gram)


def pack_kernel(at_ref, grads_ref, kept_ref, early_ref, copies_ref, moment_new_ref):
    n, width = grads_ref.shape[0], kept_ref.shape[1]
    gradient = grads_ref[0]
    for i in range(1, n):
        gradient = gradient + grads_ref[i]
    gradient = gradient / n
    moment_new = kept_ref[...] + (1.0 - BETA_ONE) * gradient
    moment_new_ref[...] = moment_new
    mine = jnp.where(at_ref[4] == 0, gradient, moment_new).astype(bf16)
    early = early_ref[...]
    for i in range(copies_ref.shape[0]):
        copies_ref[i, :, :width] = early[:, :width]
        copies_ref[i, :, width : 2 * width] = mine
        copies_ref[i, :, 2 * width :] = early[:, width:]


def pack_call(at, grads, kept, early, receivers):
    rows, width = kept.shape
    vmem = pl.BlockSpec(memory_space=pltpu.VMEM)
    shapes = [((receivers, rows, early.shape[1] + width), bf16), (kept.shape, f32)]
    return pl.pallas_call(
        pack_kernel,
        out_shape=[jax.ShapeDtypeStruct(*v) for v in shapes],
        in_specs=[pl.BlockSpec(memory_space=pltpu.SMEM)] + [vmem] * 3,
        out_specs=[vmem] * 2,
        compiler_params=pltpu.CompilerParams(vmem_limit_bytes=4 << 20),
        name="pack",
    )(at, grads, kept, early)


def local(gradients, weight, moment, second, left_gram, left_basis, right_gram, right_basis):
    n_grp = CUT[0] * CUT[1]
    rows, width = weight.shape
    right_rows = right_gram.shape[0]
    n_shard = NZ * NF * NY * NX
    deep = n_shard * rows
    core = lax.axis_index("core")
    cube = (lax.axis_index("zhi") + CUT[0] - core * (1 - lax.axis_index("zlo"))) % CUT[0]
    group = cube * CUT[1] + core
    shard = lax.axis_index(SHARD)
    row_first = shard * rows
    right_first = shard * right_rows
    first = core == 0

    grads = gather(gradients[0], GRP, n_grp)
    right_pair = right_first // rows * rows
    at = jnp.stack([right_pair, right_first - right_pair, group, row_first, core]).astype(jnp.int32)
    left_half = left_basis.astype(bf16)
    right_half = right_basis.astype(bf16)

    def fold(value, parts):
        return jnp.concatenate(jnp.split(value, parts, axis=1), axis=0)

    share = rows // n_grp
    own_second = jnp.concatenate([fold(v, 4) for v in pair(lax.dynamic_slice_in_dim(second, group * share, share, 0))], axis=0)
    start = (shard // (n_shard // BLOCKS)) * BLOCK
    round_gram = jnp.concatenate([left_gram, left_gram[:, : (SENT - 1) * BLOCK]], axis=1)
    sent_gram = lax.dynamic_slice_in_dim(round_gram, start, SENT * BLOCK, 1)
    half = deep // 2
    payload = jnp.concatenate(
        [
            jnp.where(first, left_half[:, :half], left_half[:, half:]),
            fold(jnp.where(first, right_half[:, : width // 2], right_half[:, width // 2 :]), 2),
            fold(jnp.where(first, *pair(right_gram)), 2),
            own_second,
            jnp.where(first, *pair(sent_gram)),
        ],
        axis=1,
    )
    payload, kept = lax.optimization_barrier((payload, BETA_ONE * moment))
    copies, moment_new = pack_call(at, grads, kept, payload, NXF * NF)
    payload = lax.all_to_all(copies, ("xhi", "yhi"), 0, 0)
    payload = payload.reshape((NXF, NF) + payload.shape[1:])
    cut = payload.shape[-1] - SENT * BLOCK
    near, groups = NZ * NY * NXN, cubes()
    parted = lambda v: v.reshape(NEAR + v.shape[1:])
    swap = [(0, 1), (1, 0)]
    early = gather(payload[..., :cut], AXES, near, groups)
    early_other = lax.ppermute(early, "core", swap)
    late = gather(payload[..., cut:], AXES, near, groups)

    results = mid_call(at, parted(early), parted(early_other), second, left_half, left_gram, right_gram)
    basis, outer, update, second_new, left_new, right_new, right_result = results
    update, late = lax.optimization_barrier((update, late))
    late_other = lax.ppermute(late, "core", swap)
    updates = gather(update, GRP, n_grp)
    basis, outer = (pltpu.with_memory_space_constraint(v, pltpu.HBM) for v in (basis, outer))
    left_result = left_call(at[3:], parted(late), parted(late_other), outer, basis, rows)
    updates, left_result = lax.optimization_barrier((updates, left_result))
    weight_new = weight - STEP_SIZE * jnp.sum(updates, axis=0)
    return (weight_new, moment_new, second_new, left_new, left_result, right_new, right_result)


def solution(mesh):
    cut = Mesh(mesh.devices.reshape(CUT), AXES)
    rowwise = P(SHARD, None)
    return jax.shard_map(
        local,
        mesh=cut,
        in_specs=(P(GRP, SHARD, None),) + (rowwise,) * 7,
        out_specs=(rowwise,) * 7,
        check_vma=False,
    )
```

```python
import itertools

import jax
import jax.numpy as jnp
import numpy as np
from jax import lax
from jax.experimental import pallas as pl
from jax.experimental.pallas import tpu as pltpu
from jax.sharding import Mesh, PartitionSpec as P

NS_ITERS = 2

BETA_ONE = 0.9
BETA_TWO = 0.95
GRAM_DECAY = 0.95
ADAM_EPS = 1e-08
NORM_EPS = 1e-06
STEP_SIZE = 0.02
START_SCALE = 0.75

AXES = ("zhi", "core", "zlo", "yhi", "ylo", "xhi", "xlo")
CUT = (4, 2, 2, 4, 2, 2, 2)
GRP = ("zhi", "core")
SHARD = ("zlo", "yhi", "ylo", "xhi", "xlo")
NZ, NF, NY, NXF, NXN = CUT[2:]
NX = NXF * NXN
NEAR = (NZ, NY, NXN)
bf16 = jnp.bfloat16
f32 = jnp.float32

BLOCK = 128
BLOCKS = 8
SENT = BLOCKS // 2 + 1


def mm(a, b, ca, cb):
    return lax.dot_general(a, b, (((ca,), (cb,)), ((), ())), preferred_element_type=f32)


def cubes():
    groups = []
    deep, high, wide = CUT[0] * NZ, NF * NY, NX
    for core in range(CUT[1]):
        for corner in itertools.product(range(0, deep, 2), range(0, high, 2), range(0, wide, 2)):
            group = {}
            for step in itertools.product(range(2), repeat=3):
                z, y, x = (
                    (a + core + b) % n for a, b, n in zip(corner, step, (deep, high, wide))
                )
                place = (z // NZ, core, z % NZ, y // NY, y % NY, x // NXN, x % NXN)
                group[z % NZ, y % NY, x % NXN] = int(np.ravel_multi_index(place, CUT))
            groups.append([group[k] for k in sorted(group)])
    return groups


def gather(value, axes, size, groups=None):
    copies = jnp.broadcast_to(value[None], (size,) + value.shape)
    return lax.all_to_all(copies, axes, 0, 0, axis_index_groups=groups)


def pair(value):
    high = lax.reduce_precision(value, 8, 7)
    return high.astype(bf16), (value - high).astype(bf16)


def split(value):
    high = value.astype(bf16)
    return high, (value - high.astype(f32)).astype(bf16)


def refresh(power_tile, n_tiles, tile, first, count, power, start, current, out_ref):
    sums = None
    for t in range(n_tiles):
        p = power_tile(t)
        power[pl.ds(t * tile, tile), :] = p
        s = jnp.sum(p * p, axis=0, keepdims=True)
        sums = s if sums is None else sums + s
    scale = START_SCALE / jnp.sqrt(sums + NORM_EPS)
    for t in range(n_tiles):
        at = pl.ds(t * tile, tile)
        start[at, :] = (power[at, :] * scale).astype(bf16)
    x = start[...]
    for t in range(n_tiles):
        at = pl.ds(t * tile, tile)
        mine = start[at, :]
        square = mm(mine, x, 1, 1).astype(bf16)
        current[at, :] = (1.5 * mine.astype(f32) - 0.5 * mm(square, x, 1, 0)).astype(bf16)
    x = current[...]
    rows = current[pl.ds(pl.multiple_of(first, count), count), :]
    square = mm(rows, x, 1, 1).astype(bf16)
    out_ref[...] = 1.5 * rows.astype(f32) - 0.5 * mm(square, x, 1, 0)


def left_kernel(
    first_ref, mine_hbm, other_ref, outer_hbm, basis_hbm, out_ref,
    mine_ref, basis_ref, gram, power, start, current, sems,
):
    rows, deep, tile = mine_ref.shape[-2], basis_ref.shape[0], 256
    pairs = [(mine_hbm, mine_ref), (basis_hbm, basis_ref)]
    for t in range(deep // tile):
        at = pl.ds(t * tile, tile)
        pairs.append((outer_hbm.at[at], power.at[at]))
    copies = [pltpu.make_async_copy(a, b, sems.at[i]) for i, (a, b) in enumerate(pairs)]
    for copy in copies:
        copy.start()
    copies[0].wait()
    for r in range(BLOCKS):
        zlo, far = r // NF, r % NF
        for j in range(SENT):
            c = (r + j) % BLOCKS
            at = pl.ds(j * BLOCK, BLOCK)
            pieces = []
            for near in range(NY * NX):
                y, x = near // NX, near % NX
                place = (zlo, y, x % NXN, x // NXN, far, slice(None), at)
                pieces.append(mine_ref[place].astype(f32) + other_ref[place].astype(f32))
            block = GRAM_DECAY * jnp.concatenate(pieces, axis=0)
            gram[r * BLOCK : (r + 1) * BLOCK, c * BLOCK : (c + 1) * BLOCK] = block
            if 0 < j < BLOCKS // 2:
                gram[c * BLOCK : (c + 1) * BLOCK, r * BLOCK : (r + 1) * BLOCK] = block.T
    copies[1].wait()
    basis = basis_ref[...]

    def power_tile(t):
        copies[2 + t].wait()
        at = pl.ds(t * tile, tile)
        high, low = split(gram[at, :] + power[at, :])
        return mm(high, basis, 1, 0) + mm(low, basis, 1, 0)

    refresh(power_tile, deep // tile, tile, first_ref[0], rows, power, start, current, out_ref)
    result, half = out_ref[...], deep // 2
    out_ref[...] = jnp.where(first_ref[1] == 0, result, jnp.concatenate([result[:, half:], result[:, :half]], axis=1))


def left_call(first, mine, other, outer, basis, rows):
    deep = basis.shape[0]
    hbm = pl.BlockSpec(memory_space=pltpu.HBM)
    anywhere = pl.BlockSpec(memory_space=pl.ANY)
    vmem = pl.BlockSpec(memory_space=pltpu.VMEM)
    return pl.pallas_call(
        left_kernel,
        out_shape=jax.ShapeDtypeStruct((rows, deep), f32),
        in_specs=[pl.BlockSpec(memory_space=pltpu.SMEM), anywhere, vmem, hbm, hbm],
        out_specs=vmem,
        scratch_shapes=[pltpu.VMEM(v.shape, bf16) for v in (mine, basis)]
        + [
            pltpu.VMEM((deep, deep), f32),
            pltpu.VMEM((deep, deep), f32),
            pltpu.VMEM((deep, deep), bf16),
            pltpu.VMEM((deep, deep), bf16),
            pltpu.SemaphoreType.DMA((2 + deep // 256,)),
        ],
        compiler_params=pltpu.CompilerParams(vmem_limit_bytes=28 << 20),
        cost_estimate=pl.CostEstimate(flops=10 * deep**3, transcendentals=deep, bytes_accessed=8 * deep**2),
        name="left_refresh",
    )(first, mine, other, outer, basis)


def mid_kernel(
    at_ref, mine_ref, other_ref, second_ref, left_rows_ref, left_gram_ref, right_gram_ref,
    basis_hbm, outer_hbm, update_ref, second_new_ref, left_new_ref, right_new_ref, right_out_ref,
    basis_ref, grad_ref, outer, sems, mom, right, rgram, second_rows, term, power, start, current,
):
    right_pair, right_odd, group, row_first, core = (at_ref[i] for i in range(5))
    first = core == 0
    rows, width = second_ref.shape
    deep = basis_ref.shape[0]
    half = deep // 2
    share = second_rows.shape[0] // (deep // rows)
    right_rows = rows // 2
    spot = 0
    for zlo in range(NZ):
        for far in range(NF):
            for y in range(NY):
                for x in range(NX):
                    def lanes(at, n):
                        place = (zlo, y, x % NXN, x // NXN, far, slice(None), pl.ds(at, n))
                        return mine_ref[place], other_ref[place]

                    to = pl.ds(spot * rows, rows)
                    a, b = lanes(0, half)
                    basis_ref[to, :half] = a
                    basis_ref[to, half:] = b
                    a, b = lanes(half, width)
                    grad_ref[to, :] = jnp.where(first, a, b)
                    mom[to, :] = jnp.where(first, b, a)
                    to = pl.ds(spot * right_rows, right_rows)
                    n = width // 4
                    a, b = (v.astype(f32) for v in lanes(half + width, n))
                    low, high = jnp.where(first, a, b), jnp.where(first, b, a)
                    for part in range(2):
                        of = slice(part * right_rows, (part + 1) * right_rows)
                        right[to, part * n : (part + 1) * n] = low[of]
                        right[to, (2 + part) * n : (3 + part) * n] = high[of]
                    a, b = lanes(half + width + n, 2 * n)
                    both = GRAM_DECAY * (a.astype(f32) + b.astype(f32))
                    for part in range(2):
                        of = slice(part * right_rows, (part + 1) * right_rows)
                        rgram[to, part * 2 * n : (part + 1) * 2 * n] = both[of]
                    a, _ = lanes(half + width + 3 * n, n)
                    a = a.astype(f32)
                    both = a[:right_rows] + a[right_rows:]
                    for part in range(4):
                        of = slice(part * share, (part + 1) * share)
                        second_rows[spot * share : (spot + 1) * share, part * n : (part + 1) * n] = both[of]
                    spot += 1
    copies = [
        pltpu.make_async_copy(basis_ref, basis_hbm, sems.at[0]),
        pltpu.make_async_copy(outer, outer_hbm, sems.at[1]),
    ]
    copies[0].start()
    basis, grad = basis_ref[...], grad_ref[...]
    tile = 256
    for t in range(deep // tile):
        to = pl.ds(t * tile, tile)
        outer[to, :] = (1.0 - GRAM_DECAY) * mm(grad_ref[to, :], grad, 1, 1)
    copies[1].start()
    rbasis = right[...].astype(bf16)

    n = second_rows.shape[0]
    q = lax.broadcasted_iota(jnp.int32, (1, n), 1)
    wanted = q // share * rows + group * share + q % share
    column = (lax.broadcasted_iota(jnp.int32, (deep, n), 0) + core * half) % deep
    pick = jnp.where(column == wanted, 1.0, 0.0).astype(bf16)
    q = lax.broadcasted_iota(jnp.int32, (1, n), 1)
    own = jnp.where((column == row_first + q) & (q < rows), 1.0, 0.0).astype(bf16)
    columns = mm(basis, pick, 1, 0).astype(bf16)
    own_columns = mm(basis, own, 1, 0).astype(bf16)
    rotated_grad = mm(mm(columns, grad, 0, 0).astype(bf16), rbasis, 1, 0)
    rotated_moment = mm(mm(columns, mom[...], 0, 0).astype(bf16), rbasis, 1, 0)
    own_grad = mm(mm(own_columns, grad, 0, 0).astype(bf16), rbasis, 1, 0)[:rows]
    second_part = BETA_TWO * second_rows[...] + (1.0 - BETA_TWO) * rotated_grad * rotated_grad
    second_new_ref[...] = BETA_TWO * second_ref[...] + (1.0 - BETA_TWO) * own_grad * own_grad
    direction = (rotated_moment / (jnp.sqrt(second_part) + ADAM_EPS)).astype(bf16)
    returned = mm(direction, rbasis, 1, 1).astype(bf16)
    own_rows = left_rows_ref[...]
    own_rows = jnp.where(first, own_rows, jnp.concatenate([own_rows[:, half:], own_rows[:, :half]], axis=1))
    update_ref[...] = mm(mm(own_rows, pick, 1, 0).astype(bf16), returned, 1, 0)

    own_at = pl.ds(pl.multiple_of(row_first, rows), rows)
    left_new_ref[...] = GRAM_DECAY * left_gram_ref[...] + outer[own_at, :]
    q = lax.broadcasted_iota(jnp.int32, (width, BLOCK), 1)
    column = lax.broadcasted_iota(jnp.int32, (width, BLOCK), 0)
    own = jnp.where((column == right_pair + right_odd + q) & (q < right_rows), 1.0, 0.0).astype(bf16)
    own = mm(mm(grad, own, 1, 0).astype(bf16), grad, 0, 0)[:right_rows]
    right_new_ref[...] = GRAM_DECAY * right_gram_ref[...] + (1.0 - GRAM_DECAY) * own

    def power_tile(t):
        at = pl.ds(t * tile, tile)
        whole = rgram[at, :] + (1.0 - GRAM_DECAY) * mm(grad_ref[:, t * tile : (t + 1) * tile], grad, 0, 0)
        high, low = split(whole)
        return mm(high, rbasis, 1, 0) + mm(low, rbasis, 1, 0)

    refresh(power_tile, width // tile, tile, right_pair, rows, power, start, current, term)
    right_out_ref[...] = term[pl.ds(pl.multiple_of(right_odd, right_rows), right_rows), :]
    for copy in copies:
        copy.wait()


def mid_call(at, mine, other, second, left_rows, left_gram, right_gram):
    rows, deep = left_rows.shape
    width = second.shape[1]
    vmem = pl.BlockSpec(memory_space=pltpu.VMEM)
    shapes = [
        ((deep, deep), bf16), ((deep, deep), f32), ((rows, width), f32), ((rows, width), f32),
        ((rows, deep), f32), (right_gram.shape, f32), (right_gram.shape, f32),
    ]
    return pl.pallas_call(
        mid_kernel,
        out_shape=[pltpu.HBM(*v) for v in shapes[:2]] + [jax.ShapeDtypeStruct(*v) for v in shapes[2:]],
        in_specs=[pl.BlockSpec(memory_space=pltpu.SMEM)] + [vmem] * 6,
        out_specs=[pl.BlockSpec(memory_space=pltpu.HBM)] * 2 + [vmem] * (len(shapes) - 2),
        scratch_shapes=[
            pltpu.VMEM((deep, deep), bf16),
            pltpu.VMEM((deep, width), bf16),
            pltpu.VMEM((deep, deep), f32),
            pltpu.SemaphoreType.DMA((2,)),
            pltpu.VMEM((deep, width), bf16),
            pltpu.VMEM((width, width), f32),
            pltpu.VMEM((width, width), f32),
            pltpu.VMEM((deep // (CUT[0] * CUT[1]), width), f32),
            pltpu.VMEM((rows, width), f32),
            pltpu.VMEM((width, width), f32),
            pltpu.VMEM((width, width), bf16),
            pltpu.VMEM((width, width), bf16),
        ],
        compiler_params=pltpu.CompilerParams(vmem_limit_bytes=24 << 20),
        cost_estimate=pl.CostEstimate(flops=6 * deep**3, transcendentals=width**2, bytes_accessed=12 * deep**2),
        name="middle",
    )(at, mine, other, second, left_rows, left_gram, right_gram)


def pack_kernel(at_ref, grads_ref, kept_ref, early_ref, copies_ref, moment_new_ref):
    n, width = grads_ref.shape[0], kept_ref.shape[1]
    gradient = grads_ref[0]
    for i in range(1, n):
        gradient = gradient + grads_ref[i]
    gradient = gradient / n
    moment_new = kept_ref[...] + (1.0 - BETA_ONE) * gradient
    moment_new_ref[...] = moment_new
    mine = jnp.where(at_ref[4] == 0, gradient, moment_new).astype(bf16)
    early = early_ref[...]
    for i in range(copies_ref.shape[0]):
        copies_ref[i, :, :width] = early[:, :width]
        copies_ref[i, :, width : 2 * width] = mine
        copies_ref[i, :, 2 * width :] = early[:, width:]


def pack_call(at, grads, kept, early, receivers):
    rows, width = kept.shape
    vmem = pl.BlockSpec(memory_space=pltpu.VMEM)
    shapes = [((receivers, rows, early.shape[1] + width), bf16), (kept.shape, f32)]
    return pl.pallas_call(
        pack_kernel,
        out_shape=[jax.ShapeDtypeStruct(*v) for v in shapes],
        in_specs=[pl.BlockSpec(memory_space=pltpu.SMEM)] + [vmem] * 3,
        out_specs=[vmem] * 2,
        compiler_params=pltpu.CompilerParams(vmem_limit_bytes=4 << 20),
        name="pack",
    )(at, grads, kept, early)


def local(gradients, weight, moment, second, left_gram, left_basis, right_gram, right_basis):
    n_grp = CUT[0] * CUT[1]
    rows, width = weight.shape
    right_rows = right_gram.shape[0]
    n_shard = NZ * NF * NY * NX
    deep = n_shard * rows
    core = lax.axis_index("core")
    cube = (lax.axis_index("zhi") + CUT[0] - core * (1 - lax.axis_index("zlo"))) % CUT[0]
    group = cube * CUT[1] + core
    shard = lax.axis_index(SHARD)
    row_first = shard * rows
    right_first = shard * right_rows
    first = core == 0

    grads = gather(gradients[0], GRP, n_grp)
    right_pair = right_first // rows * rows
    at = jnp.stack([right_pair, right_first - right_pair, group, row_first, core]).astype(jnp.int32)
    left_half = left_basis.astype(bf16)
    right_half = right_basis.astype(bf16)

    def fold(value, parts):
        return jnp.concatenate(jnp.split(value, parts, axis=1), axis=0)

    share = rows // n_grp
    own_second = jnp.concatenate([fold(v, 4) for v in pair(lax.dynamic_slice_in_dim(second, group * share, share, 0))], axis=0)
    start = (shard // (n_shard // BLOCKS)) * BLOCK
    round_gram = jnp.concatenate([left_gram, left_gram[:, : (SENT - 1) * BLOCK]], axis=1)
    sent_gram = lax.dynamic_slice_in_dim(round_gram, start, SENT * BLOCK, 1)
    half = deep // 2
    payload = jnp.concatenate(
        [
            jnp.where(first, left_half[:, :half], left_half[:, half:]),
            fold(jnp.where(first, right_half[:, : width // 2], right_half[:, width // 2 :]), 2),
            fold(jnp.where(first, *pair(right_gram)), 2),
            own_second,
            jnp.where(first, *pair(sent_gram)),
        ],
        axis=1,
    )
    payload, kept = lax.optimization_barrier((payload, BETA_ONE * moment))
    copies, moment_new = pack_call(at, grads, kept, payload, NXF * NF)
    payload = lax.all_to_all(copies, ("xhi", "yhi"), 0, 0)
    payload = payload.reshape((NXF, NF) + payload.shape[1:])
    cut = payload.shape[-1] - SENT * BLOCK
    near, groups = NZ * NY * NXN, cubes()
    parted = lambda v: v.reshape(NEAR + v.shape[1:])
    swap = [(0, 1), (1, 0)]
    early = gather(payload[..., :cut], AXES, near, groups)
    early_other = lax.ppermute(early, "core", swap)
    late = gather(payload[..., cut:], AXES, near, groups)

    results = mid_call(at, parted(early), parted(early_other), second, left_half, left_gram, right_gram)
    basis, outer, update, second_new, left_new, right_new, right_result = results
    update, late = lax.optimization_barrier((update, late))
    late_other = lax.ppermute(late, "core", swap)
    updates = gather(update, GRP, n_grp)
    basis, outer = (pltpu.with_memory_space_constraint(v, pltpu.HBM) for v in (basis, outer))
    left_result = left_call(at[3:], parted(late), parted(late_other), outer, basis, rows)
    updates, left_result = lax.optimization_barrier((updates, left_result))
    weight_new = weight - STEP_SIZE * jnp.sum(updates, axis=0)
    return (weight_new, moment_new, second_new, left_new, left_result, right_new, right_result)


def solution(mesh):
    cut = Mesh(mesh.devices.reshape(CUT), AXES)
    rowwise = P(SHARD, None)
    return jax.shard_map(
        local,
        mesh=cut,
        in_specs=(P(GRP, SHARD, None),) + (rowwise,) * 7,
        out_specs=(rowwise,) * 7,
        check_vma=False,
    )
```

```python
import itertools

import jax
import jax.numpy as jnp
import numpy as np
from jax import lax
from jax.experimental import pallas as pl
from jax.experimental.pallas import tpu as pltpu
from jax.sharding import Mesh, PartitionSpec as P

NS_ITERS = 2

BETA_ONE = 0.9
BETA_TWO = 0.95
GRAM_DECAY = 0.95
ADAM_EPS = 1e-08
NORM_EPS = 1e-06
STEP_SIZE = 0.02
START_SCALE = 0.75

AXES = ("zhi", "core", "zlo", "yhi", "ylo", "xhi", "xlo")
CUT = (4, 2, 2, 4, 2, 2, 2)
GRP = ("zhi", "core")
SHARD = ("zlo", "yhi", "ylo", "xhi", "xlo")
NZ, NF, NY, NXF, NXN = CUT[2:]
NX = NXF * NXN
NEAR = (NZ, NY, NXN)
bf16 = jnp.bfloat16
f32 = jnp.float32

BLOCK = 128
BLOCKS = 8
SENT = BLOCKS // 2 + 1


def mm(a, b, ca, cb):
    return lax.dot_general(a, b, (((ca,), (cb,)), ((), ())), preferred_element_type=f32)


def cubes():
    groups = []
    deep, high, wide = CUT[0] * NZ, NF * NY, NX
    for core in range(CUT[1]):
        for corner in itertools.product(range(0, deep, 2), range(0, high, 2), range(0, wide, 2)):
            group = {}
            for step in itertools.product(range(2), repeat=3):
                z, y, x = (
                    (a + core + b) % n for a, b, n in zip(corner, step, (deep, high, wide))
                )
                place = (z // NZ, core, z % NZ, y // NY, y % NY, x // NXN, x % NXN)
                group[z % NZ, y % NY, x % NXN] = int(np.ravel_multi_index(place, CUT))
            groups.append([group[k] for k in sorted(group)])
    return groups


def gather(value, axes, size, groups=None):
    copies = jnp.broadcast_to(value[None], (size,) + value.shape)
    return lax.all_to_all(copies, axes, 0, 0, axis_index_groups=groups)


def pair(value):
    high = lax.reduce_precision(value, 8, 7)
    return high.astype(bf16), (value - high).astype(bf16)


def split(value):
    high = value.astype(bf16)
    return high, (value - high.astype(f32)).astype(bf16)


def refresh(power_tile, n_tiles, tile, first, count, power, start, current, out_ref):
    sums = None
    for t in range(n_tiles):
        p = power_tile(t)
        power[pl.ds(t * tile, tile), :] = p
        s = jnp.sum(p * p, axis=0, keepdims=True)
        sums = s if sums is None else sums + s
    scale = START_SCALE / jnp.sqrt(sums + NORM_EPS)
    for t in range(n_tiles):
        at = pl.ds(t * tile, tile)
        start[at, :] = (power[at, :] * scale).astype(bf16)
    x = start[...]
    for t in range(n_tiles):
        at = pl.ds(t * tile, tile)
        mine = start[at, :]
        square = mm(mine, x, 1, 1).astype(bf16)
        current[at, :] = (1.5 * mine.astype(f32) - 0.5 * mm(square, x, 1, 0)).astype(bf16)
    x = current[...]
    rows = current[pl.ds(pl.multiple_of(first, count), count), :]
    square = mm(rows, x, 1, 1).astype(bf16)
    out_ref[...] = 1.5 * rows.astype(f32) - 0.5 * mm(square, x, 1, 0)


def left_kernel(
    first_ref, mine_hbm, other_hbm, outer_hbm, basis_hbm, out_ref,
    mine_ref, other_ref, basis_ref, gram, power, start, current, sems,
):
    rows, deep, tile = mine_ref.shape[-2], basis_ref.shape[0], 256
    part = pl.ds(mine_hbm.shape[-1] - SENT * BLOCK, SENT * BLOCK)
    lead = (slice(None),) * (len(mine_hbm.shape) - 1)
    pairs = [(mine_hbm.at[lead + (part,)], mine_ref), (other_hbm.at[lead + (part,)], other_ref), (basis_hbm, basis_ref)]
    for t in range(deep // tile):
        at = pl.ds(t * tile, tile)
        pairs.append((outer_hbm.at[at], power.at[at]))
    copies = [pltpu.make_async_copy(a, b, sems.at[i]) for i, (a, b) in enumerate(pairs)]
    for copy in copies:
        copy.start()
    copies[0].wait()
    copies[1].wait()
    for r in range(BLOCKS):
        zlo, far = r // NF, r % NF
        for j in range(SENT):
            c = (r + j) % BLOCKS
            at = pl.ds(j * BLOCK, BLOCK)
            pieces = []
            for near in range(NY * NX):
                y, x = near // NX, near % NX
                place = (zlo, y, x % NXN, x // NXN, far, slice(None), at)
                pieces.append(mine_ref[place].astype(f32) + other_ref[place].astype(f32))
            block = GRAM_DECAY * jnp.concatenate(pieces, axis=0)
            gram[r * BLOCK : (r + 1) * BLOCK, c * BLOCK : (c + 1) * BLOCK] = block
            if 0 < j < BLOCKS // 2:
                gram[c * BLOCK : (c + 1) * BLOCK, r * BLOCK : (r + 1) * BLOCK] = block.T
    copies[2].wait()
    basis = basis_ref[...]

    def power_tile(t):
        copies[3 + t].wait()
        at = pl.ds(t * tile, tile)
        high, low = split(gram[at, :] + power[at, :])
        return mm(high, basis, 1, 0) + mm(low, basis, 1, 0)

    refresh(power_tile, deep // tile, tile, first_ref[0], rows, power, start, current, out_ref)
    result, half = out_ref[...], deep // 2
    out_ref[...] = jnp.where(first_ref[1] == 0, result, jnp.concatenate([result[:, half:], result[:, :half]], axis=1))


def left_call(first, mine, other, outer, basis, rows):
    deep = basis.shape[0]
    hbm = pl.BlockSpec(memory_space=pltpu.HBM)
    vmem = pl.BlockSpec(memory_space=pltpu.VMEM)
    return pl.pallas_call(
        left_kernel,
        out_shape=jax.ShapeDtypeStruct((rows, deep), f32),
        in_specs=[pl.BlockSpec(memory_space=pltpu.SMEM)] + [hbm] * 4,
        out_specs=vmem,
        scratch_shapes=[pltpu.VMEM(mine.shape[:-1] + (SENT * BLOCK,), bf16)] * 2
        + [pltpu.VMEM(basis.shape, bf16)]
        + [
            pltpu.VMEM((deep, deep), f32),
            pltpu.VMEM((deep, deep), f32),
            pltpu.VMEM((deep, deep), bf16),
            pltpu.VMEM((deep, deep), bf16),
            pltpu.SemaphoreType.DMA((3 + deep // 256,)),
        ],
        compiler_params=pltpu.CompilerParams(vmem_limit_bytes=28 << 20),
        cost_estimate=pl.CostEstimate(flops=10 * deep**3, transcendentals=deep, bytes_accessed=8 * deep**2),
        name="left_refresh",
    )(first, mine, other, outer, basis)


def mid_kernel(
    at_ref, mine_ref, other_ref, second_ref, left_rows_ref, left_gram_ref, right_gram_ref,
    basis_hbm, outer_hbm, update_ref, second_new_ref, left_new_ref, right_new_ref, right_out_ref,
    basis_ref, grad_ref, outer, sems, mom, right, rgram, second_rows, term, power, start, current,
):
    right_pair, right_odd, group, row_first, core = (at_ref[i] for i in range(5))
    first = core == 0
    rows, width = second_ref.shape
    deep = basis_ref.shape[0]
    half = deep // 2
    share = second_rows.shape[0] // (deep // rows)
    right_rows = rows // 2
    spot = 0
    for zlo in range(NZ):
        for far in range(NF):
            for y in range(NY):
                for x in range(NX):
                    def lanes(at, n):
                        place = (zlo, y, x % NXN, x // NXN, far, slice(None), pl.ds(at, n))
                        return mine_ref[place], other_ref[place]

                    to = pl.ds(spot * rows, rows)
                    a, b = lanes(0, half)
                    basis_ref[to, :half] = a
                    basis_ref[to, half:] = b
                    a, b = lanes(half, width)
                    grad_ref[to, :] = jnp.where(first, a, b)
                    mom[to, :] = jnp.where(first, b, a)
                    to = pl.ds(spot * right_rows, right_rows)
                    n = width // 4
                    a, b = (v.astype(f32) for v in lanes(half + width, n))
                    low, high = jnp.where(first, a, b), jnp.where(first, b, a)
                    for part in range(2):
                        of = slice(part * right_rows, (part + 1) * right_rows)
                        right[to, part * n : (part + 1) * n] = low[of]
                        right[to, (2 + part) * n : (3 + part) * n] = high[of]
                    a, b = lanes(half + width + n, 2 * n)
                    both = GRAM_DECAY * (a.astype(f32) + b.astype(f32))
                    for part in range(2):
                        of = slice(part * right_rows, (part + 1) * right_rows)
                        rgram[to, part * 2 * n : (part + 1) * 2 * n] = both[of]
                    a, _ = lanes(half + width + 3 * n, n)
                    a = a.astype(f32)
                    both = a[:right_rows] + a[right_rows:]
                    for part in range(4):
                        of = slice(part * share, (part + 1) * share)
                        second_rows[spot * share : (spot + 1) * share, part * n : (part + 1) * n] = both[of]
                    spot += 1
    copies = [
        pltpu.make_async_copy(basis_ref, basis_hbm, sems.at[0]),
        pltpu.make_async_copy(outer, outer_hbm, sems.at[1]),
    ]
    copies[0].start()
    basis, grad = basis_ref[...], grad_ref[...]
    tile = 256
    for t in range(deep // tile):
        to = pl.ds(t * tile, tile)
        outer[to, :] = (1.0 - GRAM_DECAY) * mm(grad_ref[to, :], grad, 1, 1)
    copies[1].start()
    rbasis = right[...].astype(bf16)

    n = second_rows.shape[0]
    q = lax.broadcasted_iota(jnp.int32, (1, n), 1)
    wanted = q // share * rows + group * share + q % share
    column = (lax.broadcasted_iota(jnp.int32, (deep, n), 0) + core * half) % deep
    pick = jnp.where(column == wanted, 1.0, 0.0).astype(bf16)
    q = lax.broadcasted_iota(jnp.int32, (1, n), 1)
    own = jnp.where((column == row_first + q) & (q < rows), 1.0, 0.0).astype(bf16)
    columns = mm(basis, pick, 1, 0).astype(bf16)
    own_columns = mm(basis, own, 1, 0).astype(bf16)
    rotated_grad = mm(mm(columns, grad, 0, 0).astype(bf16), rbasis, 1, 0)
    rotated_moment = mm(mm(columns, mom[...], 0, 0).astype(bf16), rbasis, 1, 0)
    own_grad = mm(mm(own_columns, grad, 0, 0).astype(bf16), rbasis, 1, 0)[:rows]
    second_part = BETA_TWO * second_rows[...] + (1.0 - BETA_TWO) * rotated_grad * rotated_grad
    second_new_ref[...] = BETA_TWO * second_ref[...] + (1.0 - BETA_TWO) * own_grad * own_grad
    direction = (rotated_moment / (jnp.sqrt(second_part) + ADAM_EPS)).astype(bf16)
    returned = mm(direction, rbasis, 1, 1).astype(bf16)
    own_rows = left_rows_ref[...]
    own_rows = jnp.where(first, own_rows, jnp.concatenate([own_rows[:, half:], own_rows[:, :half]], axis=1))
    update_ref[...] = mm(mm(own_rows, pick, 1, 0).astype(bf16), returned, 1, 0)

    own_at = pl.ds(pl.multiple_of(row_first, rows), rows)
    left_new_ref[...] = GRAM_DECAY * left_gram_ref[...] + outer[own_at, :]
    q = lax.broadcasted_iota(jnp.int32, (width, BLOCK), 1)
    column = lax.broadcasted_iota(jnp.int32, (width, BLOCK), 0)
    own = jnp.where((column == right_pair + right_odd + q) & (q < right_rows), 1.0, 0.0).astype(bf16)
    own = mm(mm(grad, own, 1, 0).astype(bf16), grad, 0, 0)[:right_rows]
    right_new_ref[...] = GRAM_DECAY * right_gram_ref[...] + (1.0 - GRAM_DECAY) * own

    def power_tile(t):
        at = pl.ds(t * tile, tile)
        whole = rgram[at, :] + (1.0 - GRAM_DECAY) * mm(grad_ref[:, t * tile : (t + 1) * tile], grad, 0, 0)
        high, low = split(whole)
        return mm(high, rbasis, 1, 0) + mm(low, rbasis, 1, 0)

    refresh(power_tile, width // tile, tile, right_pair, rows, power, start, current, term)
    right_out_ref[...] = term[pl.ds(pl.multiple_of(right_odd, right_rows), right_rows), :]
    for copy in copies:
        copy.wait()


def mid_call(at, mine, other, second, left_rows, left_gram, right_gram):
    rows, deep = left_rows.shape
    width = second.shape[1]
    vmem = pl.BlockSpec(memory_space=pltpu.VMEM)
    shapes = [
        ((deep, deep), bf16), ((deep, deep), f32), ((rows, width), f32), ((rows, width), f32),
        ((rows, deep), f32), (right_gram.shape, f32), (right_gram.shape, f32),
    ]
    return pl.pallas_call(
        mid_kernel,
        out_shape=[pltpu.HBM(*v) for v in shapes[:2]] + [jax.ShapeDtypeStruct(*v) for v in shapes[2:]],
        in_specs=[pl.BlockSpec(memory_space=pltpu.SMEM)] + [vmem] * 6,
        out_specs=[pl.BlockSpec(memory_space=pltpu.HBM)] * 2 + [vmem] * (len(shapes) - 2),
        scratch_shapes=[
            pltpu.VMEM((deep, deep), bf16),
            pltpu.VMEM((deep, width), bf16),
            pltpu.VMEM((deep, deep), f32),
            pltpu.SemaphoreType.DMA((2,)),
            pltpu.VMEM((deep, width), bf16),
            pltpu.VMEM((width, width), f32),
            pltpu.VMEM((width, width), f32),
            pltpu.VMEM((deep // (CUT[0] * CUT[1]), width), f32),
            pltpu.VMEM((rows, width), f32),
            pltpu.VMEM((width, width), f32),
            pltpu.VMEM((width, width), bf16),
            pltpu.VMEM((width, width), bf16),
        ],
        compiler_params=pltpu.CompilerParams(vmem_limit_bytes=24 << 20),
        cost_estimate=pl.CostEstimate(flops=6 * deep**3, transcendentals=width**2, bytes_accessed=12 * deep**2),
        name="middle",
    )(at, mine, other, second, left_rows, left_gram, right_gram)


def pack_kernel(at_ref, grads_ref, kept_ref, early_ref, copies_ref, moment_new_ref):
    n, width = grads_ref.shape[0], kept_ref.shape[1]
    gradient = grads_ref[0]
    for i in range(1, n):
        gradient = gradient + grads_ref[i]
    gradient = gradient / n
    moment_new = kept_ref[...] + (1.0 - BETA_ONE) * gradient
    moment_new_ref[...] = moment_new
    mine = jnp.where(at_ref[4] == 0, gradient, moment_new).astype(bf16)
    early = early_ref[...]
    for i in range(copies_ref.shape[0]):
        copies_ref[i, :, :width] = early[:, :width]
        copies_ref[i, :, width : 2 * width] = mine
        copies_ref[i, :, 2 * width :] = early[:, width:]


def pack_call(at, grads, kept, early, receivers):
    rows, width = kept.shape
    vmem = pl.BlockSpec(memory_space=pltpu.VMEM)
    shapes = [((receivers, rows, early.shape[1] + width), bf16), (kept.shape, f32)]
    return pl.pallas_call(
        pack_kernel,
        out_shape=[jax.ShapeDtypeStruct(*v) for v in shapes],
        in_specs=[pl.BlockSpec(memory_space=pltpu.SMEM)] + [vmem] * 3,
        out_specs=[vmem] * 2,
        compiler_params=pltpu.CompilerParams(vmem_limit_bytes=4 << 20),
        name="pack",
    )(at, grads, kept, early)


def local(gradients, weight, moment, second, left_gram, left_basis, right_gram, right_basis):
    n_grp = CUT[0] * CUT[1]
    rows, width = weight.shape
    right_rows = right_gram.shape[0]
    n_shard = NZ * NF * NY * NX
    deep = n_shard * rows
    core = lax.axis_index("core")
    cube = (lax.axis_index("zhi") + CUT[0] - core * (1 - lax.axis_index("zlo"))) % CUT[0]
    group = cube * CUT[1] + core
    shard = lax.axis_index(SHARD)
    row_first = shard * rows
    right_first = shard * right_rows
    first = core == 0

    grads = gather(gradients[0], GRP, n_grp)
    right_pair = right_first // rows * rows
    at = jnp.stack([right_pair, right_first - right_pair, group, row_first, core]).astype(jnp.int32)
    left_half = left_basis.astype(bf16)
    right_half = right_basis.astype(bf16)

    def fold(value, parts):
        return jnp.concatenate(jnp.split(value, parts, axis=1), axis=0)

    share = rows // n_grp
    own_second = jnp.concatenate([fold(v, 4) for v in pair(lax.dynamic_slice_in_dim(second, group * share, share, 0))], axis=0)
    start = (shard // (n_shard // BLOCKS)) * BLOCK
    round_gram = jnp.concatenate([left_gram, left_gram[:, : (SENT - 1) * BLOCK]], axis=1)
    sent_gram = lax.dynamic_slice_in_dim(round_gram, start, SENT * BLOCK, 1)
    half = deep // 2
    payload = jnp.concatenate(
        [
            jnp.where(first, left_half[:, :half], left_half[:, half:]),
            fold(jnp.where(first, right_half[:, : width // 2], right_half[:, width // 2 :]), 2),
            fold(jnp.where(first, *pair(right_gram)), 2),
            own_second,
            jnp.where(first, *pair(sent_gram)),
        ],
        axis=1,
    )
    payload, kept = lax.optimization_barrier((payload, BETA_ONE * moment))
    copies, moment_new = pack_call(at, grads, kept, payload, NXF * NF)
    payload = lax.all_to_all(copies, ("xhi", "yhi"), 0, 0)
    payload = payload.reshape((NXF, NF) + payload.shape[1:])
    near, groups = NZ * NY * NXN, cubes()
    parted = lambda v: v.reshape(NEAR + v.shape[1:])
    swap = [(0, 1), (1, 0)]
    whole = parted(gather(payload, AXES, near, groups))
    other = lax.ppermute(whole, "core", swap)

    results = mid_call(at, whole, other, second, left_half, left_gram, right_gram)
    basis, outer, update, second_new, left_new, right_new, right_result = results
    updates = gather(update, GRP, n_grp)
    whole, other, basis, outer = (pltpu.with_memory_space_constraint(v, pltpu.HBM) for v in (whole, other, basis, outer))
    left_result = left_call(at[3:], whole, other, outer, basis, rows)
    updates, left_result = lax.optimization_barrier((updates, left_result))
    weight_new = weight - STEP_SIZE * jnp.sum(updates, axis=0)
    return (weight_new, moment_new, second_new, left_new, left_result, right_new, right_result)


def solution(mesh):
    cut = Mesh(mesh.devices.reshape(CUT), AXES)
    rowwise = P(SHARD, None)
    return jax.shard_map(
        local,
        mesh=cut,
        in_specs=(P(GRP, SHARD, None),) + (rowwise,) * 7,
        out_specs=(rowwise,) * 7,
        check_vma=False,
    )
```

```python
import itertools

import jax
import jax.numpy as jnp
import numpy as np
from jax import lax
from jax.experimental import pallas as pl
from jax.experimental.pallas import tpu as pltpu
from jax.sharding import Mesh, PartitionSpec as P

NS_ITERS = 2

BETA_ONE = 0.9
BETA_TWO = 0.95
GRAM_DECAY = 0.95
ADAM_EPS = 1e-08
NORM_EPS = 1e-06
STEP_SIZE = 0.02
START_SCALE = 0.75

AXES = ("zhi", "core", "zlo", "yhi", "ylo", "xhi", "xlo")
CUT = (4, 2, 2, 4, 2, 2, 2)
GRP = ("zhi", "core")
SHARD = ("zlo", "yhi", "ylo", "xhi", "xlo")
NZ, NF, NY, NXF, NXN = CUT[2:]
NX = NXF * NXN
NEAR = (NZ, NY, NXN)
bf16 = jnp.bfloat16
f32 = jnp.float32

BLOCK = 128
BLOCKS = 8
SENT = BLOCKS // 2 + 1


def mm(a, b, ca, cb):
    return lax.dot_general(a, b, (((ca,), (cb,)), ((), ())), preferred_element_type=f32)


def cubes():
    groups = []
    deep, high, wide = CUT[0] * NZ, NF * NY, NX
    for core in range(CUT[1]):
        for corner in itertools.product(range(0, deep, 2), range(0, high, 2), range(0, wide, 2)):
            group = {}
            for step in itertools.product(range(2), repeat=3):
                z, y, x = (
                    (a + core + b) % n for a, b, n in zip(corner, step, (deep, high, wide))
                )
                place = (z // NZ, core, z % NZ, y // NY, y % NY, x // NXN, x % NXN)
                group[z % NZ, y % NY, x % NXN] = int(np.ravel_multi_index(place, CUT))
            groups.append([group[k] for k in sorted(group)])
    return groups


def gather(value, axes, size, groups=None):
    copies = jnp.broadcast_to(value[None], (size,) + value.shape)
    return lax.all_to_all(copies, axes, 0, 0, axis_index_groups=groups)


def pair(value):
    high = lax.reduce_precision(value, 8, 7)
    return high.astype(bf16), (value - high).astype(bf16)


def split(value):
    high = value.astype(bf16)
    return high, (value - high.astype(f32)).astype(bf16)


def refresh(power_tile, n_tiles, tile, first, count, power, start, current, out_ref):
    sums = None
    for t in range(n_tiles):
        p = power_tile(t)
        power[pl.ds(t * tile, tile), :] = p
        s = jnp.sum(p * p, axis=0, keepdims=True)
        sums = s if sums is None else sums + s
    scale = START_SCALE / jnp.sqrt(sums + NORM_EPS)
    for t in range(n_tiles):
        at = pl.ds(t * tile, tile)
        start[at, :] = (power[at, :] * scale).astype(bf16)
    x = start[...]
    for t in range(n_tiles):
        at = pl.ds(t * tile, tile)
        mine = start[at, :]
        square = mm(mine, x, 1, 1).astype(bf16)
        current[at, :] = (1.5 * mine.astype(f32) - 0.5 * mm(square, x, 1, 0)).astype(bf16)
    x = current[...]
    rows = current[pl.ds(pl.multiple_of(first, count), count), :]
    square = mm(rows, x, 1, 1).astype(bf16)
    out_ref[...] = 1.5 * rows.astype(f32) - 0.5 * mm(square, x, 1, 0)


def left_kernel(
    first_ref, mine_hbm, other_ref, outer_hbm, basis_hbm, out_ref,
    mine_ref, basis_ref, mine_whole, other_whole, power, start, current, sems,
):
    rows, deep, tile = mine_ref.shape[-2], basis_ref.shape[0], 256
    pairs = [(mine_hbm, mine_ref), (basis_hbm, basis_ref)]
    for t in range(deep // tile):
        at = pl.ds(t * tile, tile)
        pairs.append((outer_hbm.at[at], power.at[at]))
    copies = [pltpu.make_async_copy(a, b, sems.at[i]) for i, (a, b) in enumerate(pairs)]
    for copy in copies:
        copy.start()

    def assemble(ref, whole):
        for r in range(BLOCKS):
            zlo, far = r // NF, r % NF
            for j in range(SENT):
                c = (r + j) % BLOCKS
                at = pl.ds(j * BLOCK, BLOCK)
                pieces = []
                for near in range(NY * NX):
                    y, x = near // NX, near % NX
                    pieces.append(ref[zlo, y, x % NXN, x // NXN, far, :, at])
                block = jnp.concatenate(pieces, axis=0)
                whole[r * BLOCK : (r + 1) * BLOCK, c * BLOCK : (c + 1) * BLOCK] = block
                if 0 < j < BLOCKS // 2:
                    whole[c * BLOCK : (c + 1) * BLOCK, r * BLOCK : (r + 1) * BLOCK] = block.T

    assemble(other_ref, other_whole)
    copies[0].wait()
    assemble(mine_ref, mine_whole)
    copies[1].wait()
    basis = basis_ref[...]

    def power_tile(t):
        at = pl.ds(t * tile, tile)
        p = GRAM_DECAY * (mm(other_whole[at, :], basis, 1, 0) + mm(mine_whole[at, :], basis, 1, 0))
        copies[2 + t].wait()
        return p + power[at, :]

    refresh(power_tile, deep // tile, tile, first_ref[0], rows, power, start, current, out_ref)
    result, half = out_ref[...], deep // 2
    out_ref[...] = jnp.where(first_ref[1] == 0, result, jnp.concatenate([result[:, half:], result[:, :half]], axis=1))


def left_call(first, mine, other, outer, basis, rows):
    deep = basis.shape[0]
    hbm = pl.BlockSpec(memory_space=pltpu.HBM)
    anywhere = pl.BlockSpec(memory_space=pl.ANY)
    vmem = pl.BlockSpec(memory_space=pltpu.VMEM)
    return pl.pallas_call(
        left_kernel,
        out_shape=jax.ShapeDtypeStruct((rows, deep), f32),
        in_specs=[pl.BlockSpec(memory_space=pltpu.SMEM), anywhere, vmem, hbm, hbm],
        out_specs=vmem,
        scratch_shapes=[pltpu.VMEM(v.shape, bf16) for v in (mine, basis)]
        + [
            pltpu.VMEM((deep, deep), bf16),
            pltpu.VMEM((deep, deep), bf16),
            pltpu.VMEM((deep, deep), f32),
            pltpu.VMEM((deep, deep), bf16),
            pltpu.VMEM((deep, deep), bf16),
            pltpu.SemaphoreType.DMA((2 + deep // 256,)),
        ],
        compiler_params=pltpu.CompilerParams(vmem_limit_bytes=28 << 20),
        cost_estimate=pl.CostEstimate(flops=10 * deep**3, transcendentals=deep, bytes_accessed=8 * deep**2),
        name="left_refresh",
    )(first, mine, other, outer, basis)


def mid_kernel(
    at_ref, mine_ref, other_ref, second_ref, left_rows_ref, left_gram_ref, right_gram_ref,
    basis_hbm, outer_hbm, update_ref, second_new_ref, left_new_ref, right_new_ref, right_out_ref,
    basis_ref, grad_ref, outer, sems, mom, right, rgram, second_rows, term, power, start, current,
):
    right_pair, right_odd, group, row_first, core = (at_ref[i] for i in range(5))
    first = core == 0
    rows, width = second_ref.shape
    deep = basis_ref.shape[0]
    half = deep // 2
    share = second_rows.shape[0] // (deep // rows)
    right_rows = rows // 2
    spot = 0
    for zlo in range(NZ):
        for far in range(NF):
            for y in range(NY):
                for x in range(NX):
                    def lanes(at, n):
                        place = (zlo, y, x % NXN, x // NXN, far, slice(None), pl.ds(at, n))
                        return mine_ref[place], other_ref[place]

                    to = pl.ds(spot * rows, rows)
                    a, b = lanes(0, half)
                    basis_ref[to, :half] = a
                    basis_ref[to, half:] = b
                    a, b = lanes(half, width)
                    grad_ref[to, :] = jnp.where(first, a, b)
                    mom[to, :] = jnp.where(first, b, a)
                    to = pl.ds(spot * right_rows, right_rows)
                    n = width // 4
                    a, b = (v.astype(f32) for v in lanes(half + width, n))
                    low, high = jnp.where(first, a, b), jnp.where(first, b, a)
                    for part in range(2):
                        of = slice(part * right_rows, (part + 1) * right_rows)
                        right[to, part * n : (part + 1) * n] = low[of]
                        right[to, (2 + part) * n : (3 + part) * n] = high[of]
                    a, b = lanes(half + width + n, 2 * n)
                    both = GRAM_DECAY * (a.astype(f32) + b.astype(f32))
                    for part in range(2):
                        of = slice(part * right_rows, (part + 1) * right_rows)
                        rgram[to, part * 2 * n : (part + 1) * 2 * n] = both[of]
                    a, _ = lanes(half + width + 3 * n, n)
                    a = a.astype(f32)
                    both = a[:right_rows] + a[right_rows:]
                    for part in range(4):
                        of = slice(part * share, (part + 1) * share)
                        second_rows[spot * share : (spot + 1) * share, part * n : (part + 1) * n] = both[of]
                    spot += 1
    copies = [
        pltpu.make_async_copy(basis_ref, basis_hbm, sems.at[0]),
        pltpu.make_async_copy(outer, outer_hbm, sems.at[1]),
    ]
    copies[0].start()
    basis, grad = basis_ref[...], grad_ref[...]
    tile = 256
    high, low = split((1.0 - GRAM_DECAY) * mm(grad, basis, 0, 0))
    for t in range(deep // tile):
        to = pl.ds(t * tile, tile)
        outer[to, :] = mm(grad_ref[to, :], high, 1, 0) + mm(grad_ref[to, :], low, 1, 0)
    copies[1].start()
    rbasis = right[...].astype(bf16)

    n = second_rows.shape[0]
    q = lax.broadcasted_iota(jnp.int32, (1, n), 1)
    wanted = q // share * rows + group * share + q % share
    column = (lax.broadcasted_iota(jnp.int32, (deep, n), 0) + core * half) % deep
    pick = jnp.where(column == wanted, 1.0, 0.0).astype(bf16)
    q = lax.broadcasted_iota(jnp.int32, (1, n), 1)
    own = jnp.where((column == row_first + q) & (q < rows), 1.0, 0.0).astype(bf16)
    columns = mm(basis, pick, 1, 0).astype(bf16)
    own_columns = mm(basis, own, 1, 0).astype(bf16)
    rotated_grad = mm(mm(columns, grad, 0, 0).astype(bf16), rbasis, 1, 0)
    rotated_moment = mm(mm(columns, mom[...], 0, 0).astype(bf16), rbasis, 1, 0)
    own_grad = mm(mm(own_columns, grad, 0, 0).astype(bf16), rbasis, 1, 0)[:rows]
    second_part = BETA_TWO * second_rows[...] + (1.0 - BETA_TWO) * rotated_grad * rotated_grad
    second_new_ref[...] = BETA_TWO * second_ref[...] + (1.0 - BETA_TWO) * own_grad * own_grad
    direction = (rotated_moment / (jnp.sqrt(second_part) + ADAM_EPS)).astype(bf16)
    returned = mm(direction, rbasis, 1, 1).astype(bf16)
    own_rows = left_rows_ref[...]
    own_rows = jnp.where(first, own_rows, jnp.concatenate([own_rows[:, half:], own_rows[:, :half]], axis=1))
    update_ref[...] = mm(mm(own_rows, pick, 1, 0).astype(bf16), returned, 1, 0)

    own_at = pl.ds(pl.multiple_of(row_first, rows), rows)
    left_new_ref[...] = GRAM_DECAY * left_gram_ref[...] + (1.0 - GRAM_DECAY) * mm(grad_ref[own_at, :], grad, 1, 1)
    q = lax.broadcasted_iota(jnp.int32, (width, BLOCK), 1)
    column = lax.broadcasted_iota(jnp.int32, (width, BLOCK), 0)
    own = jnp.where((column == right_pair + right_odd + q) & (q < right_rows), 1.0, 0.0).astype(bf16)
    own = mm(mm(grad, own, 1, 0).astype(bf16), grad, 0, 0)[:right_rows]
    right_new_ref[...] = GRAM_DECAY * right_gram_ref[...] + (1.0 - GRAM_DECAY) * own

    def power_tile(t):
        at = pl.ds(t * tile, tile)
        whole = rgram[at, :] + (1.0 - GRAM_DECAY) * mm(grad_ref[:, t * tile : (t + 1) * tile], grad, 0, 0)
        high, low = split(whole)
        return mm(high, rbasis, 1, 0) + mm(low, rbasis, 1, 0)

    refresh(power_tile, width // tile, tile, right_pair, rows, power, start, current, term)
    right_out_ref[...] = term[pl.ds(pl.multiple_of(right_odd, right_rows), right_rows), :]
    for copy in copies:
        copy.wait()


def mid_call(at, mine, other, second, left_rows, left_gram, right_gram):
    rows, deep = left_rows.shape
    width = second.shape[1]
    vmem = pl.BlockSpec(memory_space=pltpu.VMEM)
    shapes = [
        ((deep, deep), bf16), ((deep, deep), f32), ((rows, width), f32), ((rows, width), f32),
        ((rows, deep), f32), (right_gram.shape, f32), (right_gram.shape, f32),
    ]
    return pl.pallas_call(
        mid_kernel,
        out_shape=[pltpu.HBM(*v) for v in shapes[:2]] + [jax.ShapeDtypeStruct(*v) for v in shapes[2:]],
        in_specs=[pl.BlockSpec(memory_space=pltpu.SMEM)] + [vmem] * 6,
        out_specs=[pl.BlockSpec(memory_space=pltpu.HBM)] * 2 + [vmem] * (len(shapes) - 2),
        scratch_shapes=[
            pltpu.VMEM((deep, deep), bf16),
            pltpu.VMEM((deep, width), bf16),
            pltpu.VMEM((deep, deep), f32),
            pltpu.SemaphoreType.DMA((2,)),
            pltpu.VMEM((deep, width), bf16),
            pltpu.VMEM((width, width), f32),
            pltpu.VMEM((width, width), f32),
            pltpu.VMEM((deep // (CUT[0] * CUT[1]), width), f32),
            pltpu.VMEM((rows, width), f32),
            pltpu.VMEM((width, width), f32),
            pltpu.VMEM((width, width), bf16),
            pltpu.VMEM((width, width), bf16),
        ],
        compiler_params=pltpu.CompilerParams(vmem_limit_bytes=24 << 20),
        cost_estimate=pl.CostEstimate(flops=6 * deep**3, transcendentals=width**2, bytes_accessed=12 * deep**2),
        name="middle",
    )(at, mine, other, second, left_rows, left_gram, right_gram)


def pack_kernel(at_ref, grads_ref, kept_ref, early_ref, copies_ref, moment_new_ref):
    n, width = grads_ref.shape[0], kept_ref.shape[1]
    gradient = grads_ref[0]
    for i in range(1, n):
        gradient = gradient + grads_ref[i]
    gradient = gradient / n
    moment_new = kept_ref[...] + (1.0 - BETA_ONE) * gradient
    moment_new_ref[...] = moment_new
    mine = jnp.where(at_ref[4] == 0, gradient, moment_new).astype(bf16)
    early = early_ref[...]
    for i in range(copies_ref.shape[0]):
        copies_ref[i, :, :width] = early[:, :width]
        copies_ref[i, :, width : 2 * width] = mine
        copies_ref[i, :, 2 * width :] = early[:, width:]


def pack_call(at, grads, kept, early, receivers):
    rows, width = kept.shape
    vmem = pl.BlockSpec(memory_space=pltpu.VMEM)
    shapes = [((receivers, rows, early.shape[1] + width), bf16), (kept.shape, f32)]
    return pl.pallas_call(
        pack_kernel,
        out_shape=[jax.ShapeDtypeStruct(*v) for v in shapes],
        in_specs=[pl.BlockSpec(memory_space=pltpu.SMEM)] + [vmem] * 3,
        out_specs=[vmem] * 2,
        compiler_params=pltpu.CompilerParams(vmem_limit_bytes=4 << 20),
        name="pack",
    )(at, grads, kept, early)


def local(gradients, weight, moment, second, left_gram, left_basis, right_gram, right_basis):
    n_grp = CUT[0] * CUT[1]
    rows, width = weight.shape
    right_rows = right_gram.shape[0]
    n_shard = NZ * NF * NY * NX
    deep = n_shard * rows
    core = lax.axis_index("core")
    cube = (lax.axis_index("zhi") + CUT[0] - core * (1 - lax.axis_index("zlo"))) % CUT[0]
    group = cube * CUT[1] + core
    shard = lax.axis_index(SHARD)
    row_first = shard * rows
    right_first = shard * right_rows
    first = core == 0

    grads = gather(gradients[0], GRP, n_grp)
    right_pair = right_first // rows * rows
    at = jnp.stack([right_pair, right_first - right_pair, group, row_first, core]).astype(jnp.int32)
    left_half = left_basis.astype(bf16)
    right_half = right_basis.astype(bf16)

    def fold(value, parts):
        return jnp.concatenate(jnp.split(value, parts, axis=1), axis=0)

    share = rows // n_grp
    own_second = jnp.concatenate([fold(v, 4) for v in pair(lax.dynamic_slice_in_dim(second, group * share, share, 0))], axis=0)
    start = (shard // (n_shard // BLOCKS)) * BLOCK
    round_gram = jnp.concatenate([left_gram, left_gram[:, : (SENT - 1) * BLOCK]], axis=1)
    sent_gram = lax.dynamic_slice_in_dim(round_gram, start, SENT * BLOCK, 1)
    half = deep // 2
    payload = jnp.concatenate(
        [
            jnp.where(first, left_half[:, :half], left_half[:, half:]),
            fold(jnp.where(first, right_half[:, : width // 2], right_half[:, width // 2 :]), 2),
            fold(jnp.where(first, *pair(right_gram)), 2),
            own_second,
            jnp.where(first, *pair(sent_gram)),
        ],
        axis=1,
    )
    payload, kept = lax.optimization_barrier((payload, BETA_ONE * moment))
    copies, moment_new = pack_call(at, grads, kept, payload, NXF * NF)
    payload = lax.all_to_all(copies, ("xhi", "yhi"), 0, 0)
    payload = payload.reshape((NXF, NF) + payload.shape[1:])
    cut = payload.shape[-1] - SENT * BLOCK
    near, groups = NZ * NY * NXN, cubes()
    parted = lambda v: v.reshape(NEAR + v.shape[1:])
    swap = [(0, 1), (1, 0)]
    early = gather(payload[..., :cut], AXES, near, groups)
    early_other = lax.ppermute(early, "core", swap)
    late = gather(payload[..., cut:], AXES, near, groups)

    results = mid_call(at, parted(early), parted(early_other), second, left_half, left_gram, right_gram)
    basis, outer, update, second_new, left_new, right_new, right_result = results
    update, late = lax.optimization_barrier((update, late))
    late_other = lax.ppermute(late, "core", swap)
    updates = gather(update, GRP, n_grp)
    basis, outer = (pltpu.with_memory_space_constraint(v, pltpu.HBM) for v in (basis, outer))
    left_result = left_call(at[3:], parted(late), parted(late_other), outer, basis, rows)
    updates, left_result = lax.optimization_barrier((updates, left_result))
    weight_new = weight - STEP_SIZE * sum(updates[i] for i in range(n_grp))
    return (weight_new, moment_new, second_new, left_new, left_result, right_new, right_result)


def solution(mesh):
    cut = Mesh(mesh.devices.reshape(CUT), AXES)
    rowwise = P(SHARD, None)
    return jax.shard_map(
        local,
        mesh=cut,
        in_specs=(P(GRP, SHARD, None),) + (rowwise,) * 7,
        out_specs=(rowwise,) * 7,
        check_vma=False,
    )
```

```python
import itertools

import jax
import jax.numpy as jnp
import numpy as np
from jax import lax
from jax.experimental import pallas as pl
from jax.experimental.pallas import tpu as pltpu
from jax.sharding import Mesh, PartitionSpec as P

NS_ITERS = 2

BETA_ONE = 0.9
BETA_TWO = 0.95
GRAM_DECAY = 0.95
ADAM_EPS = 1e-08
NORM_EPS = 1e-06
STEP_SIZE = 0.02
START_SCALE = 0.75

AXES = ("zhi", "core", "zlo", "yhi", "ylo", "xhi", "xlo")
CUT = (4, 2, 2, 4, 2, 2, 2)
GRP = ("zhi", "core")
SHARD = ("zlo", "yhi", "ylo", "xhi", "xlo")
NZ, NF, NY, NXF, NXN = CUT[2:]
NX = NXF * NXN
NEAR = (NZ, NY, NXN)
bf16 = jnp.bfloat16
f32 = jnp.float32

BLOCK = 128
BLOCKS = 8
SENT = BLOCKS // 2 + 1


def mm(a, b, ca, cb):
    return lax.dot_general(a, b, (((ca,), (cb,)), ((), ())), preferred_element_type=f32)


def cubes():
    groups = []
    deep, high, wide = CUT[0] * NZ, NF * NY, NX
    for core in range(CUT[1]):
        for corner in itertools.product(range(0, deep, 2), range(0, high, 2), range(0, wide, 2)):
            group = {}
            for step in itertools.product(range(2), repeat=3):
                z, y, x = (
                    (a + core + b) % n for a, b, n in zip(corner, step, (deep, high, wide))
                )
                place = (z // NZ, core, z % NZ, y // NY, y % NY, x // NXN, x % NXN)
                group[z % NZ, y % NY, x % NXN] = int(np.ravel_multi_index(place, CUT))
            groups.append([group[k] for k in sorted(group)])
    return groups


def gather(value, axes, size, groups=None):
    copies = jnp.broadcast_to(value[None], (size,) + value.shape)
    return lax.all_to_all(copies, axes, 0, 0, axis_index_groups=groups)


def pair(value):
    high = lax.reduce_precision(value, 8, 7)
    return high.astype(bf16), (value - high).astype(bf16)


def split(value):
    high = value.astype(bf16)
    return high, (value - high.astype(f32)).astype(bf16)


def refresh(power_tile, n_tiles, tile, first, count, power, start, current, out_ref):
    sums = None
    for t in range(n_tiles):
        p = power_tile(t)
        power[pl.ds(t * tile, tile), :] = p
        s = jnp.sum(p * p, axis=0, keepdims=True)
        sums = s if sums is None else sums + s
    scale = START_SCALE / jnp.sqrt(sums + NORM_EPS)
    for t in range(n_tiles):
        at = pl.ds(t * tile, tile)
        start[at, :] = (power[at, :] * scale).astype(bf16)
    x = start[...]
    for t in range(n_tiles):
        at = pl.ds(t * tile, tile)
        mine = start[at, :]
        square = mm(mine, x, 1, 1).astype(bf16)
        current[at, :] = (1.5 * mine.astype(f32) - 0.5 * mm(square, x, 1, 0)).astype(bf16)
    x = current[...]
    rows = current[pl.ds(pl.multiple_of(first, count), count), :]
    square = mm(rows, x, 1, 1).astype(bf16)
    out_ref[...] = 1.5 * rows.astype(f32) - 0.5 * mm(square, x, 1, 0)


def left_kernel(
    first_ref, mine_hbm, other_ref, outer_hbm, basis_hbm, out_ref,
    mine_ref, basis_ref, gram, power, start, current, sems,
):
    rows, deep, tile = mine_ref.shape[-2], basis_ref.shape[0], 256
    pairs = [(mine_hbm.at[z], mine_ref.at[z]) for z in range(NZ)] + [(basis_hbm, basis_ref)]
    for t in range(deep // tile):
        at = pl.ds(t * tile, tile)
        pairs.append((outer_hbm.at[at], power.at[at]))
    copies = [pltpu.make_async_copy(a, b, sems.at[i]) for i, (a, b) in enumerate(pairs)]
    for copy in copies:
        copy.start()
    for r in range(BLOCKS):
        zlo, far = r // NF, r % NF
        if far == 0:
            copies[zlo].wait()
        for j in range(SENT):
            c = (r + j) % BLOCKS
            at = pl.ds(j * BLOCK, BLOCK)
            pieces = []
            for near in range(NY * NX):
                y, x = near // NX, near % NX
                place = (zlo, y, x % NXN, x // NXN, far, slice(None), at)
                pieces.append(mine_ref[place].astype(f32) + other_ref[place].astype(f32))
            block = GRAM_DECAY * jnp.concatenate(pieces, axis=0)
            gram[r * BLOCK : (r + 1) * BLOCK, c * BLOCK : (c + 1) * BLOCK] = block
            if 0 < j < BLOCKS // 2:
                gram[c * BLOCK : (c + 1) * BLOCK, r * BLOCK : (r + 1) * BLOCK] = block.T
    copies[NZ].wait()
    basis = basis_ref[...]

    def power_tile(t):
        copies[NZ + 1 + t].wait()
        at = pl.ds(t * tile, tile)
        high, low = split(gram[at, :] + power[at, :])
        return mm(high, basis, 1, 0) + mm(low, basis, 1, 0)

    refresh(power_tile, deep // tile, tile, first_ref[0], rows, power, start, current, out_ref)
    result, half = out_ref[...], deep // 2
    out_ref[...] = jnp.where(first_ref[1] == 0, result, jnp.concatenate([result[:, half:], result[:, :half]], axis=1))


def left_call(first, mine, other, outer, basis, rows):
    deep = basis.shape[0]
    hbm = pl.BlockSpec(memory_space=pltpu.HBM)
    anywhere = pl.BlockSpec(memory_space=pl.ANY)
    vmem = pl.BlockSpec(memory_space=pltpu.VMEM)
    return pl.pallas_call(
        left_kernel,
        out_shape=jax.ShapeDtypeStruct((rows, deep), f32),
        in_specs=[pl.BlockSpec(memory_space=pltpu.SMEM), anywhere, vmem, hbm, hbm],
        out_specs=vmem,
        scratch_shapes=[pltpu.VMEM(v.shape, bf16) for v in (mine, basis)]
        + [
            pltpu.VMEM((deep, deep), f32),
            pltpu.VMEM((deep, deep), f32),
            pltpu.VMEM((deep, deep), bf16),
            pltpu.VMEM((deep, deep), bf16),
            pltpu.SemaphoreType.DMA((NZ + 1 + deep // 256,)),
        ],
        compiler_params=pltpu.CompilerParams(vmem_limit_bytes=28 << 20),
        cost_estimate=pl.CostEstimate(flops=10 * deep**3, transcendentals=deep, bytes_accessed=8 * deep**2),
        name="left_refresh",
    )(first, mine, other, outer, basis)


def mid_kernel(
    at_ref, mine_ref, other_ref, second_ref, left_rows_ref, left_gram_ref, right_gram_ref,
    basis_hbm, outer_hbm, update_ref, second_new_ref, left_new_ref, right_new_ref, right_out_ref,
    basis_ref, grad_ref, outer, sems, mom, right, rgram, second_rows, term, power, start, current,
):
    right_pair, right_odd, group, row_first, core = (at_ref[i] for i in range(5))
    first = core == 0
    rows, width = second_ref.shape
    deep = basis_ref.shape[0]
    half = deep // 2
    share = second_rows.shape[0] // (deep // rows)
    right_rows = rows // 2
    spot = 0
    for zlo in range(NZ):
        for far in range(NF):
            for y in range(NY):
                for x in range(NX):
                    def lanes(at, n):
                        place = (zlo, y, x % NXN, x // NXN, far, slice(None), pl.ds(at, n))
                        return mine_ref[place], other_ref[place]

                    to = pl.ds(spot * rows, rows)
                    a, b = lanes(0, half)
                    basis_ref[to, :half] = a
                    basis_ref[to, half:] = b
                    a, b = lanes(half, width)
                    grad_ref[to, :] = jnp.where(first, a, b)
                    mom[to, :] = jnp.where(first, b, a)
                    to = pl.ds(spot * right_rows, right_rows)
                    n = width // 4
                    a, b = (v.astype(f32) for v in lanes(half + width, n))
                    low, high = jnp.where(first, a, b), jnp.where(first, b, a)
                    for part in range(2):
                        of = slice(part * right_rows, (part + 1) * right_rows)
                        right[to, part * n : (part + 1) * n] = low[of]
                        right[to, (2 + part) * n : (3 + part) * n] = high[of]
                    a, b = lanes(half + width + n, 2 * n)
                    both = GRAM_DECAY * (a.astype(f32) + b.astype(f32))
                    for part in range(2):
                        of = slice(part * right_rows, (part + 1) * right_rows)
                        rgram[to, part * 2 * n : (part + 1) * 2 * n] = both[of]
                    a, _ = lanes(half + width + 3 * n, n)
                    a = a.astype(f32)
                    both = a[:right_rows] + a[right_rows:]
                    for part in range(4):
                        of = slice(part * share, (part + 1) * share)
                        second_rows[spot * share : (spot + 1) * share, part * n : (part + 1) * n] = both[of]
                    spot += 1
    copies = [
        pltpu.make_async_copy(basis_ref, basis_hbm, sems.at[0]),
        pltpu.make_async_copy(outer, outer_hbm, sems.at[1]),
    ]
    copies[0].start()
    basis, grad = basis_ref[...], grad_ref[...]
    tile = 256
    for t in range(deep // tile):
        to = pl.ds(t * tile, tile)
        outer[to, :] = (1.0 - GRAM_DECAY) * mm(grad_ref[to, :], grad, 1, 1)
    copies[1].start()
    rbasis = right[...].astype(bf16)

    n = second_rows.shape[0]
    q = lax.broadcasted_iota(jnp.int32, (1, n), 1)
    wanted = q // share * rows + group * share + q % share
    column = (lax.broadcasted_iota(jnp.int32, (deep, n), 0) + core * half) % deep
    pick = jnp.where(column == wanted, 1.0, 0.0).astype(bf16)
    q = lax.broadcasted_iota(jnp.int32, (1, n), 1)
    own = jnp.where((column == row_first + q) & (q < rows), 1.0, 0.0).astype(bf16)
    columns = mm(basis, pick, 1, 0).astype(bf16)
    own_columns = mm(basis, own, 1, 0).astype(bf16)
    rotated_grad = mm(mm(columns, grad, 0, 0).astype(bf16), rbasis, 1, 0)
    rotated_moment = mm(mm(columns, mom[...], 0, 0).astype(bf16), rbasis, 1, 0)
    own_grad = mm(mm(own_columns, grad, 0, 0).astype(bf16), rbasis, 1, 0)[:rows]
    second_part = BETA_TWO * second_rows[...] + (1.0 - BETA_TWO) * rotated_grad * rotated_grad
    second_new_ref[...] = BETA_TWO * second_ref[...] + (1.0 - BETA_TWO) * own_grad * own_grad
    direction = (rotated_moment / (jnp.sqrt(second_part) + ADAM_EPS)).astype(bf16)
    returned = mm(direction, rbasis, 1, 1).astype(bf16)
    own_rows = left_rows_ref[...]
    own_rows = jnp.where(first, own_rows, jnp.concatenate([own_rows[:, half:], own_rows[:, :half]], axis=1))
    update_ref[...] = mm(mm(own_rows, pick, 1, 0).astype(bf16), returned, 1, 0)

    own_at = pl.ds(pl.multiple_of(row_first, rows), rows)
    left_new_ref[...] = GRAM_DECAY * left_gram_ref[...] + outer[own_at, :]
    q = lax.broadcasted_iota(jnp.int32, (width, BLOCK), 1)
    column = lax.broadcasted_iota(jnp.int32, (width, BLOCK), 0)
    own = jnp.where((column == right_pair + right_odd + q) & (q < right_rows), 1.0, 0.0).astype(bf16)
    own = mm(mm(grad, own, 1, 0).astype(bf16), grad, 0, 0)[:right_rows]
    right_new_ref[...] = GRAM_DECAY * right_gram_ref[...] + (1.0 - GRAM_DECAY) * own

    def power_tile(t):
        at = pl.ds(t * tile, tile)
        whole = rgram[at, :] + (1.0 - GRAM_DECAY) * mm(grad_ref[:, t * tile : (t + 1) * tile], grad, 0, 0)
        high, low = split(whole)
        return mm(high, rbasis, 1, 0) + mm(low, rbasis, 1, 0)

    refresh(power_tile, width // tile, tile, right_pair, rows, power, start, current, term)
    right_out_ref[...] = term[pl.ds(pl.multiple_of(right_odd, right_rows), right_rows), :]
    for copy in copies:
        copy.wait()


def mid_call(at, mine, other, second, left_rows, left_gram, right_gram):
    rows, deep = left_rows.shape
    width = second.shape[1]
    vmem = pl.BlockSpec(memory_space=pltpu.VMEM)
    shapes = [
        ((deep, deep), bf16), ((deep, deep), f32), ((rows, width), f32), ((rows, width), f32),
        ((rows, deep), f32), (right_gram.shape, f32), (right_gram.shape, f32),
    ]
    return pl.pallas_call(
        mid_kernel,
        out_shape=[pltpu.HBM(*v) for v in shapes[:2]] + [jax.ShapeDtypeStruct(*v) for v in shapes[2:]],
        in_specs=[pl.BlockSpec(memory_space=pltpu.SMEM)] + [vmem] * 6,
        out_specs=[pl.BlockSpec(memory_space=pltpu.HBM)] * 2 + [vmem] * (len(shapes) - 2),
        scratch_shapes=[
            pltpu.VMEM((deep, deep), bf16),
            pltpu.VMEM((deep, width), bf16),
            pltpu.VMEM((deep, deep), f32),
            pltpu.SemaphoreType.DMA((2,)),
            pltpu.VMEM((deep, width), bf16),
            pltpu.VMEM((width, width), f32),
            pltpu.VMEM((width, width), f32),
            pltpu.VMEM((deep // (CUT[0] * CUT[1]), width), f32),
            pltpu.VMEM((rows, width), f32),
            pltpu.VMEM((width, width), f32),
            pltpu.VMEM((width, width), bf16),
            pltpu.VMEM((width, width), bf16),
        ],
        compiler_params=pltpu.CompilerParams(vmem_limit_bytes=24 << 20),
        cost_estimate=pl.CostEstimate(flops=6 * deep**3, transcendentals=width**2, bytes_accessed=12 * deep**2),
        name="middle",
    )(at, mine, other, second, left_rows, left_gram, right_gram)


def pack_kernel(at_ref, grads_ref, kept_ref, early_ref, copies_ref, moment_new_ref):
    n, width = grads_ref.shape[0], kept_ref.shape[1]
    gradient = grads_ref[0]
    for i in range(1, n):
        gradient = gradient + grads_ref[i]
    gradient = gradient / n
    moment_new = kept_ref[...] + (1.0 - BETA_ONE) * gradient
    moment_new_ref[...] = moment_new
    mine = jnp.where(at_ref[4] == 0, gradient, moment_new).astype(bf16)
    early = early_ref[...]
    for i in range(copies_ref.shape[0]):
        copies_ref[i, :, :width] = early[:, :width]
        copies_ref[i, :, width : 2 * width] = mine
        copies_ref[i, :, 2 * width :] = early[:, width:]


def pack_call(at, grads, kept, early, receivers):
    rows, width = kept.shape
    vmem = pl.BlockSpec(memory_space=pltpu.VMEM)
    shapes = [((receivers, rows, early.shape[1] + width), bf16), (kept.shape, f32)]
    return pl.pallas_call(
        pack_kernel,
        out_shape=[jax.ShapeDtypeStruct(*v) for v in shapes],
        in_specs=[pl.BlockSpec(memory_space=pltpu.SMEM)] + [vmem] * 3,
        out_specs=[vmem] * 2,
        compiler_params=pltpu.CompilerParams(vmem_limit_bytes=4 << 20),
        name="pack",
    )(at, grads, kept, early)


def local(gradients, weight, moment, second, left_gram, left_basis, right_gram, right_basis):
    n_grp = CUT[0] * CUT[1]
    rows, width = weight.shape
    right_rows = right_gram.shape[0]
    n_shard = NZ * NF * NY * NX
    deep = n_shard * rows
    core = lax.axis_index("core")
    cube = (lax.axis_index("zhi") + CUT[0] - core * (1 - lax.axis_index("zlo"))) % CUT[0]
    group = cube * CUT[1] + core
    shard = lax.axis_index(SHARD)
    row_first = shard * rows
    right_first = shard * right_rows
    first = core == 0

    grads = gather(gradients[0], GRP, n_grp)
    right_pair = right_first // rows * rows
    at = jnp.stack([right_pair, right_first - right_pair, group, row_first, core]).astype(jnp.int32)
    left_half = left_basis.astype(bf16)
    right_half = right_basis.astype(bf16)

    def fold(value, parts):
        return jnp.concatenate(jnp.split(value, parts, axis=1), axis=0)

    share = rows // n_grp
    own_second = jnp.concatenate([fold(v, 4) for v in pair(lax.dynamic_slice_in_dim(second, group * share, share, 0))], axis=0)
    start = (shard // (n_shard // BLOCKS)) * BLOCK
    round_gram = jnp.concatenate([left_gram, left_gram[:, : (SENT - 1) * BLOCK]], axis=1)
    sent_gram = lax.dynamic_slice_in_dim(round_gram, start, SENT * BLOCK, 1)
    half = deep // 2
    payload = jnp.concatenate(
        [
            jnp.where(first, left_half[:, :half], left_half[:, half:]),
            fold(jnp.where(first, right_half[:, : width // 2], right_half[:, width // 2 :]), 2),
            fold(jnp.where(first, *pair(right_gram)), 2),
            own_second,
            jnp.where(first, *pair(sent_gram)),
        ],
        axis=1,
    )
    payload, kept = lax.optimization_barrier((payload, BETA_ONE * moment))
    copies, moment_new = pack_call(at, grads, kept, payload, NXF * NF)
    payload = lax.all_to_all(copies, ("xhi", "yhi"), 0, 0)
    payload = payload.reshape((NXF, NF) + payload.shape[1:])
    cut = payload.shape[-1] - SENT * BLOCK
    near, groups = NZ * NY * NXN, cubes()
    parted = lambda v: v.reshape(NEAR + v.shape[1:])
    swap = [(0, 1), (1, 0)]
    early = gather(payload[..., :cut], AXES, near, groups)
    early_other = lax.ppermute(early, "core", swap)
    late = gather(payload[..., cut:], AXES, near, groups)

    results = mid_call(at, parted(early), parted(early_other), second, left_half, left_gram, right_gram)
    basis, outer, update, second_new, left_new, right_new, right_result = results
    update, late = lax.optimization_barrier((update, late))
    late_other = lax.ppermute(late, "core", swap)
    updates = gather(update, GRP, n_grp)
    basis, outer = (pltpu.with_memory_space_constraint(v, pltpu.HBM) for v in (basis, outer))
    left_result = left_call(at[3:], parted(late), parted(late_other), outer, basis, rows)
    updates, left_result = lax.optimization_barrier((updates, left_result))
    weight_new = weight - STEP_SIZE * sum(updates[i] for i in range(n_grp))
    return (weight_new, moment_new, second_new, left_new, left_result, right_new, right_result)


def solution(mesh):
    cut = Mesh(mesh.devices.reshape(CUT), AXES)
    rowwise = P(SHARD, None)
    return jax.shard_map(
        local,
        mesh=cut,
        in_specs=(P(GRP, SHARD, None),) + (rowwise,) * 7,
        out_specs=(rowwise,) * 7,
        check_vma=False,
    )
```
